128 devices in a mesh: ctx: 16 (over x, y), tp: 8 (over z, core).
Axes of the slice: x: 4, y: 4, z: 4, core: 2. Of those that a mesh axis runs over, the one named last changes fastest.
Arguments:
- main_q: bfloat16 [7168, 24576], P('ctx', 'tp'), may hold values from -6 to 6
- main_k: bfloat16 [2048, 24576], P('ctx', 'tp'), may hold values from -6 to 6
- log_norms: float32 [7168, 128], P('ctx', 'tp'), may hold values from 0 to 4
- index_q: bfloat16 [7168, 64, 128], P(('ctx', 'tp')), may hold values from -8 to 8
- index_w: float32 [7168, 64], P(('ctx', 'tp')), may hold values from -2 to 2
- index_k: bfloat16 [2048, 128], P('ctx'), may hold values from -8 to 8
- row_weight: float32 [7168], P(('ctx', 'tp')), may hold values from 10 to 200
- offsets: int32 [16], P('ctx'), may hold values from 0 to 1600
- key_map: int32 [16], replicated, may hold values from 0 to 15, as said below
Outputs:
- grad_index_q: float32 [7168, 64, 128], P(('ctx', 'tp'))
- grad_index_w: float32 [7168, 64], P(('ctx', 'tp'))
- grad_index_k: float32 [2048, 128], P(('ctx', 'tp'))
The draws below stay inside these ranges and needn't reach their ends.
Inputs may be any that keep to these rules, and one draw needn't show every extreme that they name: `key_map`: each key block number appears exactly once.
All inputs are finite; a program needn't handle non-finite values.
Results may differ from the reference program's by a relative error of at most 0.0028.
Values may be sent and summed in bfloat16 or wider, within the bound.
A program may use at most 128 MiB of HBM per device.

```python
import math
import jax
import jax.numpy as jnp
from jax import lax

H = 128
DQK = 192
HI = 64
DI = 128
Q_DEV = 448
KEY_DEV = 128
BLOCKS = 16
QUERIES = 7168
KEYS = 2048
N_TP = 8


def drawn_normal(key, shape, limit):
    return jnp.clip(jax.random.normal(key, shape, jnp.float32), -limit, limit)


def row_scales(key, count, low, high):
    return jnp.exp(jax.random.uniform(key, (count, 1), jnp.float32, math.log(low), math.log(high)))


def main_values(key, count):
    common = drawn_normal(jax.random.fold_in(key, 1), (count, 1, DQK), 4.0)
    own = drawn_normal(jax.random.fold_in(key, 2), (count, H, DQK), 4.0)
    values = 1.41 * common + 0.71 * own
    return jnp.clip(values, -6.0, 6.0).reshape(count, H * DQK)


def draw_main_q(key, part):
    return main_values(jax.random.fold_in(key, 21), QUERIES).astype(jnp.bfloat16)


def draw_main_k(key, part):
    return main_values(jax.random.fold_in(key, 22), KEYS).astype(jnp.bfloat16)


def indexer_parts(key):
    key_map = jax.random.permutation(jax.random.fold_in(key, 11), BLOCKS).astype(jnp.int32)
    weights = 0.3 * drawn_normal(jax.random.fold_in(key, 12), (QUERIES, HI), 4.0)
    key_noise = drawn_normal(jax.random.fold_in(key, 13), (KEYS, DI), 4.0)
    query_noise = drawn_normal(jax.random.fold_in(key, 14), (QUERIES, HI, DI), 4.0)
    index_k = key_noise * row_scales(jax.random.fold_in(key, 17), KEYS, 0.25, 2.5)
    index_q = query_noise * row_scales(jax.random.fold_in(key, 18), QUERIES, 0.4, 1.2)[:, :, None]
    index_q = jnp.clip(index_q, -8.0, 8.0)
    index_k = jnp.clip(index_k, -8.0, 8.0)
    weights = jnp.clip(weights, -2.0, 2.0)
    return (key_map, index_q, index_k, weights)


def draw_key_map(key, part):
    return indexer_parts(key)[0]


def draw_index_q(key, part):
    return indexer_parts(key)[1].astype(jnp.bfloat16)


def draw_index_k(key, part):
    return indexer_parts(key)[2].astype(jnp.bfloat16)


def draw_index_w(key, part):
    return indexer_parts(key)[3]


def plant(drawn, stream_key, least, top_value):
    longest = drawn.shape.index(max(drawn.shape))
    spots = []
    for shift in (0, 1):
        where = [jax.random.randint(jax.random.fold_in(stream_key, axis), (), 0, length) for axis, length in enumerate(drawn.shape)]
        where[longest] = (where[longest] + shift) % drawn.shape[longest]
        spots.append(tuple(where))
    return drawn.at[spots[0]].set(least).at[spots[1]].set(top_value)


def level_of(stream_key, dims, pieces, least, largest):
    factor_of, own = 1.0, jax.random.fold_in(stream_key, 6)
    for dim, blocks in pieces:
        steps = jnp.exp(jax.random.uniform(jax.random.fold_in(own, dim), (blocks,), jnp.float32, least / len(pieces), largest / len(pieces)))
        factor_of = factor_of * jnp.repeat(steps, dims[dim] // blocks).reshape([-1 if axis == dim else 1 for axis in range(len(dims))])
    return factor_of


def setup_inputs(seed: int = 0) -> dict:
    arg_keys = jax.random.split(jax.random.key(seed), 10)
    main_q = draw_main_q(jax.random.fold_in(arg_keys[9], 71), 0)
    main_k = draw_main_k(jax.random.fold_in(arg_keys[9], 71), 0)
    log_norms = jnp.clip(4.0 * jax.random.uniform(arg_keys[2], (QUERIES, H), jnp.float32) ** level_of(arg_keys[2], (QUERIES, H), ((0, 16), (1, 8)), -0.2, 0.2), 0.0, 4.0)
    index_q = draw_index_q(jax.random.fold_in(arg_keys[9], 71), 0)
    index_w = draw_index_w(jax.random.fold_in(arg_keys[9], 71), 0)
    index_k = draw_index_k(jax.random.fold_in(arg_keys[9], 71), 0)
    row_weight = jnp.clip(jnp.exp(math.log(200.0) - 2.9957323 * jax.random.uniform(arg_keys[6], (QUERIES,), jnp.float32) ** level_of(arg_keys[6], (QUERIES,), ((0, 128),), -0.2, 0.2)), 10.0, 200.0)
    offsets = plant(jax.random.randint(arg_keys[7], (BLOCKS,), 0, KEYS - Q_DEV + 1), jax.random.fold_in(arg_keys[7], 1), 0, KEYS - Q_DEV).astype(jnp.int32)
    key_map = draw_key_map(jax.random.fold_in(arg_keys[9], 71), 0)
    return {"main_q": main_q, "main_k": main_k, "log_norms": log_norms, "index_q": index_q, "index_w": index_w, "index_k": index_k, "row_weight": row_weight, "offsets": offsets, "key_map": key_map}


def reference(main_q, main_k, log_norms, index_q, index_w, index_k, row_weight, offsets, key_map):
    own_rows = Q_DEV // N_TP
    block_count = QUERIES // own_rows
    storage = jnp.arange(KEYS, dtype=jnp.int32)
    key_pos = key_map[storage // KEY_DEV] * KEY_DEV + storage % KEY_DEV
    query_rows = jnp.arange(QUERIES, dtype=jnp.int32)
    query_pos = offsets[query_rows // Q_DEV] + query_rows % Q_DEV
    keys_wide = main_k.astype(jnp.float32).reshape(KEYS, H, DQK)
    index_keys = index_k.astype(jnp.float32)
    score_scale = 1.0 / math.sqrt(DQK)
    inv_root = 1.0 / math.sqrt(DI)

    def one_block(running, number):
        first_row = (number * own_rows).astype(jnp.int32)
        queries = lax.dynamic_slice_in_dim(main_q, first_row, own_rows, 0).astype(jnp.float32).reshape(own_rows, H, DQK)
        norm_rows = lax.dynamic_slice_in_dim(log_norms, first_row, own_rows, 0)
        row_pos = lax.dynamic_slice_in_dim(query_pos, first_row, own_rows, 0)
        visible = key_pos[None, :] <= row_pos[:, None]
        scores = jnp.einsum('qhd,khd->qhk', queries, keys_wide) * score_scale
        prob_terms = jnp.where(visible[:, None, :], jnp.exp(scores - norm_rows[:, :, None]), 0.0)
        head_mass = lax.optimization_barrier(jnp.sum(prob_terms, axis=1))
        target = head_mass / lax.optimization_barrier(jnp.sum(head_mass, axis=1, keepdims=True))
        index_rows = lax.dynamic_slice_in_dim(index_q, first_row, own_rows, 0).astype(jnp.float32)
        weight_rows = lax.dynamic_slice_in_dim(index_w, first_row, own_rows, 0)
        loss_rows = lax.dynamic_slice_in_dim(row_weight, first_row, own_rows, 0)
        inner = jnp.einsum('tjd,kd->tjk', index_rows, index_keys) * inv_root
        logits = lax.optimization_barrier(jnp.sum(weight_rows[:, :, None] * jax.nn.softplus(inner), axis=1))
        masked = jnp.where(visible, logits, -jnp.inf)
        row_max = lax.optimization_barrier(jnp.max(masked, axis=1, keepdims=True))
        exp_terms = jnp.exp(masked - row_max)
        index_probs = exp_terms / lax.optimization_barrier(jnp.sum(exp_terms, axis=1, keepdims=True))
        logit_grad = loss_rows[:, None] * (index_probs - target)
        grad_w = lax.optimization_barrier(jnp.sum(logit_grad[:, None, :] * jax.nn.softplus(inner), axis=2))
        score_grad = (logit_grad[:, None, :] * weight_rows[:, :, None] * jax.nn.sigmoid(inner) * inv_root).astype(jnp.bfloat16)
        score_wide = score_grad.astype(jnp.float32)
        grad_q = jnp.einsum('tjk,kd->tjd', score_wide, index_keys)
        running = running + jnp.einsum('tjk,tjd->kd', score_wide, index_rows)
        return (running, (grad_q, grad_w))
    grad_k, stacked = lax.scan(one_block, jnp.zeros((KEYS, DI), jnp.float32), jnp.arange(block_count, dtype=jnp.int32))
    grad_q = stacked[0].reshape(QUERIES, HI, DI)
    grad_w = stacked[1].reshape(QUERIES, HI)
    return (grad_q, grad_w, grad_k)
```

```python
import math

import jax
import jax.numpy as jnp
from jax import lax
from jax.experimental import pallas as pl
from jax.experimental.pallas import tpu as pltpu
from jax.sharding import PartitionSpec as P

MESH = pl.DeviceIdType.MESH
SIDE = 4
N_CTX = SIDE * SIDE
N_TP = 8
ROWS = 448
KEYS = 128
DQK = 192
HEADS = 16
OWN = 56
HI = 64
DI = 128
FLAT = OWN * HI
WIDE = 256
LOG2E = math.log2(math.e)
LN2 = math.log(2.0)
VMEM_LIMIT = 67043328
CONTRACT_LAST = (((1,), (1,)), ((), ()))


def rem(a, b):
    return lax.rem(a, jnp.int32(b))


def div(a, b):
    return lax.div(a, jnp.int32(b))


def ring_places(ctx):
    x, y = div(ctx, SIDE), rem(ctx, SIDE)
    turn = rem(x + y, SIDE)
    return SIDE * x + turn, SIDE * y + turn


def ring_member(ring, place):
    place = rem(place + 2 * N_CTX, N_CTX)
    major = div(place, SIDE)
    minor = rem(rem(place, SIDE) - major + SIDE, SIDE)
    return SIDE * major + minor if ring < 2 else SIDE * minor + major


def kernel(
    q_hbm, k_hbm, norm_hbm, iq_hbm, iw_ref, ik_hbm, rw_ref, off_ref, map_ref,
    gq_hbm, gw_ref, gk_ref,
    qpad, kbuf, ikbuf, iq, iqt, norm, nb, wb, nsp, lg, mass, mrecv, gkt, gkst, grk, fst, frecv,
    lsem, qsem, ksend, isend, krecv, irecv, msend, mrsem, gsend, gsem, fsend, fsem, osem,
):
    ctx, tp = lax.axis_index("ctx"), lax.axis_index("tp")
    place1, place2 = ring_places(ctx)
    places = (place1, place1, place2, place2)
    turns = (1, -1, 1, -1)
    nexts = [ring_member(i, places[i] + turns[i]) for i in range(4)]

    def source(ring, slot):
        return ring_member(ring, places[ring] - turns[ring] * slot)

    local = [
        pltpu.make_async_copy(k_hbm, kbuf.at[0], lsem.at[0]),
        pltpu.make_async_copy(ik_hbm, ikbuf.at[0], lsem.at[1]),
        pltpu.make_async_copy(norm_hbm, norm, lsem.at[2]),
        pltpu.make_async_copy(iq_hbm, iq, lsem.at[3]),
    ]
    for copy in local:
        copy.start()
    q_copies = []
    for head in range(HEADS):
        first = (head // 2) * 2 * DQK + (head % 2) * 128
        q_copies.append(
            pltpu.make_async_copy(q_hbm.at[:, pl.ds(first, WIDE)], qpad.at[head], qsem.at[head])
        )
        q_copies[-1].start()

    barrier = pltpu.get_barrier_semaphore()

    def greet_ctx(d, carry):
        pl.semaphore_signal(
            barrier, inc=1, device_id={"ctx": rem(ctx + d, N_CTX)}, device_id_type=MESH
        )
        return carry

    def greet_tp(d, carry):
        pl.semaphore_signal(
            barrier, inc=1, device_id={"tp": rem(tp + d, N_TP)}, device_id_type=MESH
        )
        return carry

    lax.fori_loop(1, N_CTX, greet_ctx, 0)
    lax.fori_loop(1, N_TP, greet_tp, 0)
    pl.semaphore_wait(barrier, N_CTX + N_TP - 2)

    def send_keys(slot, half):
        for i in range(4):
            pltpu.make_async_remote_copy(
                src_ref=kbuf.at[slot, half, i],
                dst_ref=kbuf.at[slot + 1, half, i],
                send_sem=ksend,
                recv_sem=krecv.at[slot + 1, half],
                device_id={"ctx": nexts[i]},
                device_id_type=MESH,
            ).start()

    def send_index_keys(slot):
        for i in range(4):
            pltpu.make_async_remote_copy(
                src_ref=ikbuf.at[slot, :, i],
                dst_ref=ikbuf.at[slot + 1, :, i],
                send_sem=isend,
                recv_sem=irecv.at[slot + 1],
                device_id={"ctx": nexts[i]},
                device_id_type=MESH,
            ).start()

    def wait_keys(slot, half):
        pltpu.make_async_copy(kbuf.at[slot, half], kbuf.at[slot, half], krecv.at[slot, half]).wait()

    def wait_index_keys(slot):
        pltpu.make_async_copy(ikbuf.at[slot], ikbuf.at[slot], irecv.at[slot]).wait()

    local[1].wait()
    send_index_keys(0)
    local[0].wait()
    send_keys(0, 0)
    send_keys(0, 1)

    for copy in local[2:]:
        copy.wait()
    for copy in q_copies:
        copy.wait()
    lane = lax.broadcasted_iota(jnp.int32, (ROWS, 128), 1)
    for head in range(HEADS):
        cols = slice(128, 256) if head % 2 == 0 else slice(0, 128)
        kept = lane < DQK - 128 if head % 2 == 0 else lane >= 256 - DQK
        part = jnp.where(kept, qpad[head, :, cols].astype(jnp.float32), 0.0)
        qpad[head, :, cols] = part.astype(jnp.bfloat16)
        nb[head * ROWS : (head + 1) * ROWS, :] = jnp.broadcast_to(
            norm[:, head : head + 1] * LOG2E, (ROWS, 128)
        )

    diagonal = lax.broadcasted_iota(jnp.int32, (HI, HI), 0) == lax.broadcasted_iota(
        jnp.int32, (HI, HI), 1
    )

    def spread_weights(t, carry):
        row = jnp.broadcast_to(iw_ref[pl.ds(t, 1), :], (HI, HI))
        column = jnp.sum(jnp.where(diagonal, row, 0.0), axis=1, keepdims=True)
        wb[pl.ds(pl.multiple_of(t * HI, HI), HI), :] = jnp.broadcast_to(column, (HI, 128))
        return carry

    lax.fori_loop(0, OWN, spread_weights, 0)

    def turn_queries(b, carry):
        first = pl.multiple_of(b * WIDE, WIDE)
        iqt[:, pl.ds(first, WIDE)] = iq[pl.ds(first, WIDE), :].astype(jnp.float32).T.astype(jnp.bfloat16)
        return carry

    lax.fori_loop(0, FLAT // WIDE, turn_queries, 0)

    score_scale = LOG2E / math.sqrt(DQK)
    inv_root = 1.0 / math.sqrt(DI)
    half_rows = ROWS // 2

    def head_mass(slot, half, parity):
        first = pl.multiple_of(half * half_rows, half_rows)
        total = None
        for head in range(HEADS):
            col = (head // 2) * 2 * DQK + (head % 2) * 128
            keys = kbuf[slot, :, :, :, col : col + WIDE].reshape(KEYS, WIDE)
            scores = lax.dot_general(
                qpad[head, pl.ds(first, half_rows), :], keys, CONTRACT_LAST,
                preferred_element_type=jnp.float32,
            )
            norms = nb[pl.ds(pl.multiple_of(head * ROWS + first, 32), half_rows), :]
            term = jnp.exp2(scores * score_scale - norms)
            total = term if total is None else total + term
        mass[parity, pl.ds(first, half_rows), :] = total

    def first_pass(slot, half):
        keys = ikbuf[slot].reshape(KEYS, DI)

        def eight_rows(b, carry):
            rows = []
            for part in range(2):
                first = pl.multiple_of(b * 8 * HI + part * 4 * HI, 4 * HI)
                inner = lax.dot_general(
                    iq[pl.ds(first, 4 * HI), :], keys, CONTRACT_LAST,
                    preferred_element_type=jnp.float32,
                )
                v = inner * (inv_root * LOG2E)
                minus = jnp.minimum(-v, 0.0) - jnp.log2(1.0 + jnp.exp2(-jnp.abs(v)))
                nsp[slot, pl.ds(first, 4 * HI), :] = minus
                weighted = wb[pl.ds(first, 4 * HI), :] * minus
                for u in range(4):
                    rows.append(
                        jnp.sum(weighted[u * HI : (u + 1) * HI, :], axis=0, keepdims=True)
                    )
            lg[slot, pl.ds(pl.multiple_of(b * 8, 8), 8), :] = jnp.concatenate(rows, axis=0)
            return carry

        lax.fori_loop(4 * half, 4 + 3 * half, eight_rows, 0)

    def wait_mass_sent(parity):
        sent = mass.at[parity, pl.ds(0, ROWS - OWN)]
        pltpu.make_async_copy(sent, sent, msend.at[parity]).wait()

    def send_mass(slot, parity):
        for d in range(1, N_TP):
            peer = rem(tp + d, N_TP)
            pltpu.make_async_remote_copy(
                src_ref=mass.at[parity, pl.ds(pl.multiple_of(peer * OWN, 8), OWN)],
                dst_ref=mrecv.at[d, slot],
                send_sem=msend.at[parity],
                recv_sem=mrsem,
                device_id={"tp": peer},
                device_id_type=MESH,
            ).start()
        mrecv[0, slot] = mass[parity, pl.ds(pl.multiple_of(tp * OWN, 8), OWN), :]

    def step(it, carry):
        slot, half = div(it, 2), rem(it, 2)

        @pl.when(it < 2 * (N_CTX - 1))
        def _():
            @pl.when(half == 0)
            def _():
                wait_index_keys(slot)
                send_index_keys(slot)

            wait_keys(slot, half)
            send_keys(slot, half)

        @pl.when(it == 2 * N_CTX)
        def _():
            wait_index_keys(N_CTX - 1)
            wait_keys(N_CTX - 1, 0)
            wait_keys(N_CTX - 1, 1)

        now = slot - 1
        parity = rem(now, 2)

        @pl.when((half == 0) & (now >= 2))
        def _():
            wait_mass_sent(parity)

        head_mass(now, half, parity)

        @pl.when(half == 1)
        def _():
            send_mass(now, parity)

        first_pass(now, half)
        return carry

    lax.fori_loop(2, 2 * N_CTX + 2, step, 0)

    lane_row = lax.broadcasted_iota(jnp.int32, (OWN, 128), 1)
    row_pos = off_ref[0] + tp * OWN + lax.broadcasted_iota(jnp.int32, (OWN, 128), 0)
    ring_lane = rem(lax.broadcasted_iota(jnp.int32, (OWN, 128), 1), 64)

    def visible_at(slot):
        blocks = [map_ref[source(i, slot)] * KEYS for i in range(4)]
        block = jnp.where(
            ring_lane < 32,
            jnp.where(ring_lane < 16, blocks[0], blocks[1]),
            jnp.where(ring_lane < 48, blocks[2], blocks[3]),
        )
        return block + lane_row <= row_pos

    def take_max(slot, top):
        masked = jnp.where(visible_at(slot), -lg[slot], -jnp.inf)
        lg[slot] = masked
        return jnp.maximum(top, masked)

    top = lax.fori_loop(0, N_CTX, take_max, jnp.full((OWN, 128), -jnp.inf, jnp.float32))
    top = jnp.max(top, axis=1, keepdims=True)

    def take_exp(slot, total):
        term = jnp.exp2(lg[slot] - top)
        lg[slot] = term
        return total + term

    exp_total = lax.fori_loop(0, N_CTX, take_exp, jnp.zeros((OWN, 128), jnp.float32))
    exp_share = 1.0 / jnp.sum(exp_total, axis=1, keepdims=True)

    arrived = mrecv.at[pl.ds(1, N_TP - 1)]
    pltpu.make_async_copy(arrived, arrived, mrsem).wait()

    def add_mass(slot, total):
        amount = mrecv[0, slot]
        for d in range(1, N_TP):
            amount = amount + mrecv[d, slot]
        amount = jnp.where(visible_at(slot), amount, 0.0)
        mrecv[0, slot] = amount
        return total + amount

    mass_total = lax.fori_loop(0, N_CTX, add_mass, jnp.zeros((OWN, 128), jnp.float32))
    mass_total = jnp.sum(mass_total, axis=1, keepdims=True)

    def take_grad(slot, carry):
        lg[slot] = lg[slot] * exp_share - mrecv[0, slot] / mass_total
        return carry

    lax.fori_loop(0, N_CTX, take_grad, 0)

    nb[...] = jnp.zeros_like(nb)

    def key_pair(pair, carry):
        slot_a, slot_b = 2 * pair, 2 * pair + 1
        keys = ikbuf[pl.ds(slot_a, 2)].reshape(2 * KEYS, DI)
        gkt[...] = jnp.zeros_like(gkt)

        def row_block(b, carry):
            first = pl.multiple_of(b * WIDE, WIDE)
            pieces = []
            for u in range(4):
                t = b * 4 + u
                at = pl.multiple_of(first + u * HI, HI)
                weight = rw_ref[t]
                grad_a = lg[slot_a, pl.ds(t, 1), :] * weight
                grad_b = lg[slot_b, pl.ds(t, 1), :] * weight
                heads = wb[pl.ds(at, HI), :] * inv_root
                soft_a = nsp[slot_a, pl.ds(at, HI), :]
                soft_b = nsp[slot_b, pl.ds(at, HI), :]
                lanes = pl.ds(pl.multiple_of(FLAT + at, HI), HI)
                nb[lanes, :] += grad_a * soft_a + grad_b * soft_b
                part_a = (grad_a * heads) * (1.0 - jnp.exp2(soft_a))
                part_b = (grad_b * heads) * (1.0 - jnp.exp2(soft_b))
                pieces.append(
                    jnp.concatenate(
                        [part_a.astype(jnp.bfloat16), part_b.astype(jnp.bfloat16)], axis=1
                    )
                )
            score_grad = jnp.concatenate(pieces, axis=0)
            nb[pl.ds(first, WIDE), :] += jnp.dot(
                score_grad, keys, preferred_element_type=jnp.float32
            )
            gkt[...] += jnp.dot(
                iqt[:, pl.ds(first, WIDE)], score_grad, preferred_element_type=jnp.float32
            )
            return carry

        lax.fori_loop(0, FLAT // WIDE, row_block, 0)
        for part, slot in ((0, slot_a), (1, slot_b)):
            turned = gkt[:, part * KEYS : (part + 1) * KEYS].T.reshape(2, 4, 16, DI)
            gkst[slot] = turned

            def send(slot=slot):
                for i in range(4):
                    pltpu.make_async_remote_copy(
                        src_ref=gkst.at[slot, :, i],
                        dst_ref=grk.at[slot, :, i],
                        send_sem=gsend,
                        recv_sem=gsem,
                        device_id={"ctx": source(i, slot)},
                        device_id_type=MESH,
                    ).start()

            if part == 0:
                pl.when(pair > 0)(send)
            else:
                send()
        return carry

    lax.fori_loop(0, N_CTX // 2, key_pair, 0)
    out_copy = pltpu.make_async_copy(nb.at[pl.ds(0, FLAT)], gq_hbm, osem)
    out_copy.start()

    def finish_weights(r, carry):
        block = nb[pl.ds(pl.multiple_of(FLAT + r * 128, 128), 128), :]
        gw_ref[pl.ds(r, 1), :] = jnp.sum(block.T, axis=0, keepdims=True) * -LN2
        return carry

    lax.fori_loop(0, FLAT // 128, finish_weights, 0)

    came = grk.at[pl.ds(1, N_CTX - 1)]
    pltpu.make_async_copy(came, came, gsem).wait()
    own_sum = gkst[0]
    for slot in range(1, N_CTX):
        own_sum = own_sum + grk[slot]
    fst[...] = own_sum.reshape(N_TP, 16, DI)
    for d in range(1, N_TP):
        peer = rem(tp + d, N_TP)
        pltpu.make_async_remote_copy(
            src_ref=fst.at[peer],
            dst_ref=frecv.at[d],
            send_sem=fsend,
            recv_sem=fsem,
            device_id={"tp": peer},
            device_id_type=MESH,
        ).start()
    landed = frecv.at[pl.ds(1, N_TP - 1)]
    pltpu.make_async_copy(landed, landed, fsem).wait()
    total = fst[tp]
    for d in range(1, N_TP):
        total = total + frecv[d]
    gk_ref[...] = total

    out_copy.wait()
    pltpu.make_async_copy(landed, landed, fsend).wait()
    sent = kbuf.at[pl.ds(0, N_CTX - 1)]
    pltpu.make_async_copy(sent, sent, ksend).wait()
    sent = ikbuf.at[pl.ds(0, N_CTX - 1)]
    pltpu.make_async_copy(sent, sent, isend).wait()
    pltpu.make_async_copy(came, came, gsend).wait()
    wait_mass_sent(0)
    wait_mass_sent(1)


def per_device(main_q, main_k, log_norms, index_q, index_w, index_k, row_weight, offsets, key_map):
    anywhere = pl.BlockSpec(memory_space=pl.ANY)
    vmem = pl.BlockSpec(memory_space=pltpu.VMEM)
    smem = pl.BlockSpec(memory_space=pltpu.SMEM)
    f32, bf16 = jnp.float32, jnp.bfloat16
    dma = pltpu.SemaphoreType.DMA
    grad_q, grad_w, grad_k = pl.pallas_call(
        kernel,
        out_shape=(
            jax.ShapeDtypeStruct((FLAT, DI), f32),
            jax.ShapeDtypeStruct((FLAT // 128, 128), f32),
            jax.ShapeDtypeStruct((16, DI), f32),
        ),
        in_specs=[anywhere, anywhere, anywhere, anywhere, vmem, anywhere, smem, smem, smem],
        out_specs=(anywhere, vmem, vmem),
        scratch_shapes=[
            pltpu.VMEM((HEADS, ROWS, WIDE), bf16),
            pltpu.VMEM((N_CTX, 2, 4, 16, HEADS * DQK), bf16),
            pltpu.VMEM((N_CTX, 2, 4, 16, DI), bf16),
            pltpu.VMEM((FLAT, DI), bf16),
            pltpu.VMEM((DI, FLAT), bf16),
            pltpu.VMEM((ROWS, HEADS), f32),
            pltpu.VMEM((HEADS * ROWS, 128), f32),
            pltpu.VMEM((FLAT, 128), f32),
            pltpu.VMEM((N_CTX, FLAT, 128), f32),
            pltpu.VMEM((N_CTX, OWN, 128), f32),
            pltpu.VMEM((2, ROWS, 128), f32),
            pltpu.VMEM((N_TP, N_CTX, OWN, 128), f32),
            pltpu.VMEM((DI, 2 * KEYS), f32),
            pltpu.VMEM((N_CTX, 2, 4, 16, DI), f32),
            pltpu.VMEM((N_CTX, 2, 4, 16, DI), f32),
            pltpu.VMEM((N_TP, 16, DI), f32),
            pltpu.VMEM((N_TP, 16, DI), f32),
            dma((4,)),
            dma((HEADS,)),
            dma,
            dma,
            dma((N_CTX, 2)),
            dma((N_CTX,)),
            dma((2,)),
            dma,
            dma,
            dma,
            dma,
            dma,
            dma,
        ],
        compiler_params=pltpu.CompilerParams(
            collective_id=0, has_side_effects=True, vmem_limit_bytes=VMEM_LIMIT
        ),
        name="indexer_grads",
    )(
        main_q,
        main_k.reshape(2, 4, 16, HEADS * DQK),
        log_norms,
        index_q.reshape(FLAT, DI),
        index_w,
        index_k.reshape(2, 4, 16, DI),
        row_weight,
        offsets,
        key_map,
    )
    return grad_q.reshape(OWN, HI, DI), grad_w.reshape(OWN, HI), grad_k


def solution(mesh):
    placed = (
        P("ctx", "tp"),
        P("ctx", "tp"),
        P("ctx", "tp"),
        P(("ctx", "tp"), None, None),
        P(("ctx", "tp"), None),
        P("ctx", None),
        P(("ctx", "tp")),
        P("ctx"),
        P(),
    )
    return jax.shard_map(
        per_device,
        mesh=mesh,
        in_specs=placed,
        out_specs=(P(("ctx", "tp"), None, None), P(("ctx", "tp"), None), P(("ctx", "tp"), None)),
        check_vma=False,
    )
```

```python
import math

import jax
import jax.numpy as jnp
from jax import lax
from jax.experimental import pallas as pl
from jax.experimental.pallas import tpu as pltpu
from jax.sharding import PartitionSpec as P

MESH = pl.DeviceIdType.MESH
SIDE = 4
N_CTX = SIDE * SIDE
N_TP = 8
ROWS = 448
KEYS = 128
DQK = 192
HEADS = 16
OWN = 56
HI = 64
DI = 128
FLAT = OWN * HI
WIDE = 256
BLOCK = 512
PIECES = 4
LOG2E = math.log2(math.e)
LN2 = math.log(2.0)
VMEM_LIMIT = 67043328
CONTRACT_LAST = (((1,), (1,)), ((), ()))


def rem(a, b):
    return lax.rem(a, jnp.int32(b))


def div(a, b):
    return lax.div(a, jnp.int32(b))


def ring_places(ctx):
    x, y = div(ctx, SIDE), rem(ctx, SIDE)
    turn = rem(x + y, SIDE)
    return SIDE * x + turn, SIDE * y + turn


def ring_member(ring, place):
    place = rem(place + 2 * N_CTX, N_CTX)
    major = div(place, SIDE)
    minor = rem(rem(place, SIDE) - major + SIDE, SIDE)
    return SIDE * major + minor if ring < 2 else SIDE * minor + major


def kernel(
    q_hbm, k_hbm, norm_hbm, iq_hbm, iw_ref, ik_hbm, rw_ref, off_ref, map_ref,
    gq_hbm, gw_ref, gk_ref,
    qpad, kbuf, ikbuf, iq, iqt, norm, nb, wb, nsp, lg, mass, mrecv, gkt, gkst, grk, fst, frecv,
    lsem, qsem, ksend, isend, krecv, irecv, msend, mrsem, gsend, gsem, fsend, fsem, osem,
):
    ctx, tp = lax.axis_index("ctx"), lax.axis_index("tp")
    place1, place2 = ring_places(ctx)
    places = (place1, place1, place2, place2)
    turns = (1, -1, 1, -1)
    nexts = [ring_member(i, places[i] + turns[i]) for i in range(4)]

    def source(ring, slot):
        return ring_member(ring, places[ring] - turns[ring] * slot)

    local = [
        pltpu.make_async_copy(k_hbm, kbuf.at[0], lsem.at[0]),
        pltpu.make_async_copy(ik_hbm, ikbuf.at[0], lsem.at[1]),
        pltpu.make_async_copy(norm_hbm, norm, lsem.at[2]),
        pltpu.make_async_copy(iq_hbm, iq, lsem.at[3]),
    ]
    for copy in local:
        copy.start()
    q_copies = []
    for head in range(HEADS):
        first = (head // 2) * 2 * DQK + (head % 2) * 128
        q_copies.append(
            pltpu.make_async_copy(q_hbm.at[:, pl.ds(first, WIDE)], qpad.at[head], qsem.at[head])
        )
        q_copies[-1].start()

    barrier = pltpu.get_barrier_semaphore()

    def greet_tp(d, carry):
        pl.semaphore_signal(
            barrier, inc=1, device_id={"tp": rem(tp + d, N_TP)}, device_id_type=MESH
        )
        return carry

    for i in range(4):
        pl.semaphore_signal(barrier, inc=1, device_id={"ctx": nexts[i]}, device_id_type=MESH)
    lax.fori_loop(1, N_TP, greet_tp, 0)
    pl.semaphore_wait(barrier, 4 + N_TP - 1)

    def send_keys(slot, half):
        for i in range(4):
            pltpu.make_async_remote_copy(
                src_ref=kbuf.at[slot, half, i],
                dst_ref=kbuf.at[slot + 1, half, i],
                send_sem=ksend,
                recv_sem=krecv.at[slot + 1, half],
                device_id={"ctx": nexts[i]},
                device_id_type=MESH,
            ).start()

    def send_index_keys(slot):
        for i in range(4):
            pltpu.make_async_remote_copy(
                src_ref=ikbuf.at[slot, :, i],
                dst_ref=ikbuf.at[slot + 1, :, i],
                send_sem=isend,
                recv_sem=irecv.at[slot + 1],
                device_id={"ctx": nexts[i]},
                device_id_type=MESH,
            ).start()

    def wait_keys(slot, half):
        pltpu.make_async_copy(kbuf.at[slot, half], kbuf.at[slot, half], krecv.at[slot, half]).wait()

    def wait_index_keys(slot):
        pltpu.make_async_copy(ikbuf.at[slot], ikbuf.at[slot], irecv.at[slot]).wait()

    local[1].wait()
    send_index_keys(0)
    local[0].wait()
    send_keys(0, 0)
    send_keys(0, 1)

    for copy in local[2:]:
        copy.wait()
    for copy in q_copies:
        copy.wait()
    lane = lax.broadcasted_iota(jnp.int32, (ROWS, 128), 1)
    norms_down = norm[...].T * LOG2E
    for head in range(HEADS):
        cols = slice(128, 256) if head % 2 == 0 else slice(0, 128)
        kept = lane < DQK - 128 if head % 2 == 0 else lane >= 256 - DQK
        part = jnp.where(kept, qpad[head, :, cols].astype(jnp.float32), 0.0)
        qpad[head, :, cols] = part.astype(jnp.bfloat16)
        nb[head * ROWS : (head + 1) * ROWS, :] = jnp.broadcast_to(
            norms_down[:, head : head + 1], (ROWS, 128)
        )
    weights_down = iw_ref[...].T
    for t in range(OWN):
        wb[t * HI : (t + 1) * HI, :] = jnp.broadcast_to(weights_down[:, t : t + 1], (HI, 128))

    def turn_queries(b, carry):
        first = pl.multiple_of(b * WIDE, WIDE)
        iqt[:, pl.ds(first, WIDE)] = iq[pl.ds(first, WIDE), :].astype(jnp.float32).T.astype(jnp.bfloat16)
        return carry


    score_scale = LOG2E / math.sqrt(DQK)
    inv_root = 1.0 / math.sqrt(DI)
    half_rows = ROWS // 2

    def head_mass(slot, half, parity):
        first = pl.multiple_of(half * half_rows, half_rows)
        total = None
        for head in range(HEADS):
            col = (head // 2) * 2 * DQK + (head % 2) * 128
            keys = kbuf[slot, :, :, :, col : col + WIDE].reshape(KEYS, WIDE)
            scores = lax.dot_general(
                qpad[head, pl.ds(first, half_rows), :], keys, CONTRACT_LAST,
                preferred_element_type=jnp.float32,
            )
            norms = nb[pl.ds(pl.multiple_of(head * ROWS + first, 32), half_rows), :]
            term = jnp.exp2(scores * score_scale - norms)
            total = term if total is None else total + term
        mass[parity, pl.ds(first, half_rows), :] = total

    def first_pass(slot):
        keys = ikbuf[slot].reshape(KEYS, DI)

        def eight_rows(b, carry):
            rows = []
            for part in range(2):
                first = pl.multiple_of(b * 8 * HI + part * 4 * HI, 4 * HI)
                inner = lax.dot_general(
                    iq[pl.ds(first, 4 * HI), :], keys, CONTRACT_LAST,
                    preferred_element_type=jnp.float32,
                )
                v = inner * (inv_root * LOG2E)
                minus = jnp.minimum(-v, 0.0) - jnp.log2(1.0 + jnp.exp2(-jnp.abs(v)))
                nsp[slot, pl.ds(first, 4 * HI), :] = minus
                weighted = wb[pl.ds(first, 4 * HI), :] * minus
                for u in range(4):
                    rows.append(
                        jnp.sum(weighted[u * HI : (u + 1) * HI, :], axis=0, keepdims=True)
                    )
            lg[slot, pl.ds(pl.multiple_of(b * 8, 8), 8), :] = jnp.concatenate(rows, axis=0)
            return carry

        lax.fori_loop(0, OWN // 8, eight_rows, 0, unroll=7)

    def wait_mass_sent(parity):
        sent = mass.at[parity, pl.ds(0, ROWS - OWN)]
        pltpu.make_async_copy(sent, sent, msend.at[parity]).wait()

    def send_mass(slot, parity):
        for d in range(1, N_TP):
            peer = rem(tp + d, N_TP)
            pltpu.make_async_remote_copy(
                src_ref=mass.at[parity, pl.ds(pl.multiple_of(peer * OWN, 8), OWN)],
                dst_ref=mrecv.at[d, slot],
                send_sem=msend.at[parity],
                recv_sem=mrsem,
                device_id={"tp": peer},
                device_id_type=MESH,
            ).start()
        mrecv[0, slot] = mass[parity, pl.ds(pl.multiple_of(tp * OWN, 8), OWN), :]

    def step(it, carry):
        slot, half = div(it, 2), rem(it, 2)

        @pl.when(it < 2 * (N_CTX - 1))
        def _():
            @pl.when(half == 0)
            def _():
                wait_index_keys(slot)
                send_index_keys(slot)

            wait_keys(slot, half)
            send_keys(slot, half)

        @pl.when(it == 2 * N_CTX)
        def _():
            wait_index_keys(N_CTX - 1)
            wait_keys(N_CTX - 1, 0)
            wait_keys(N_CTX - 1, 1)

        now = slot - 1
        parity = rem(now, 2)

        @pl.when((half == 0) & (now >= 2))
        def _():
            wait_mass_sent(parity)

        head_mass(now, half, parity)

        @pl.when(half == 1)
        def _():
            send_mass(now, parity)

        @pl.when(now == 0)
        def _():
            lax.fori_loop(7 * half, 7 + 7 * half, turn_queries, 0)

        @pl.when((half == 1) & (now > 0))
        def _():
            first_pass(now - 1)

        return carry

    lax.fori_loop(2, 2 * N_CTX + 2, step, 0)
    first_pass(N_CTX - 1)

    lane_row = lax.broadcasted_iota(jnp.int32, (OWN, 128), 1)
    row_pos = off_ref[0] + tp * OWN + lax.broadcasted_iota(jnp.int32, (OWN, 128), 0)
    ring_lane = rem(lax.broadcasted_iota(jnp.int32, (OWN, 128), 1), 64)

    def visible_at(slot):
        blocks = [map_ref[source(i, slot)] * KEYS for i in range(4)]
        block = jnp.where(
            ring_lane < 32,
            jnp.where(ring_lane < 16, blocks[0], blocks[1]),
            jnp.where(ring_lane < 48, blocks[2], blocks[3]),
        )
        return block + lane_row <= row_pos

    def take_max(slot, top):
        masked = jnp.where(visible_at(slot), -lg[slot], -jnp.inf)
        lg[slot] = masked
        return jnp.maximum(top, masked)

    top = lax.fori_loop(0, N_CTX, take_max, jnp.full((OWN, 128), -jnp.inf, jnp.float32))
    top = jnp.max(top, axis=1, keepdims=True)

    def take_exp(slot, total):
        term = jnp.exp2(lg[slot] - top)
        lg[slot] = term
        return total + term

    exp_total = lax.fori_loop(0, N_CTX, take_exp, jnp.zeros((OWN, 128), jnp.float32))
    exp_share = 1.0 / jnp.sum(exp_total, axis=1, keepdims=True)

    nb[...] = jnp.zeros_like(nb)
    arrived = mrecv.at[pl.ds(1, N_TP - 1)]
    pltpu.make_async_copy(arrived, arrived, mrsem).wait()

    def add_mass(slot, total):
        amount = mrecv[0, slot]
        for d in range(1, N_TP):
            amount = amount + mrecv[d, slot]
        amount = jnp.where(visible_at(slot), amount, 0.0)
        mrecv[0, slot] = amount
        return total + amount

    mass_total = lax.fori_loop(0, N_CTX, add_mass, jnp.zeros((OWN, 128), jnp.float32))
    mass_total = jnp.sum(mass_total, axis=1, keepdims=True)

    def take_grad(slot, carry):
        lg[slot] = lg[slot] * exp_share - mrecv[0, slot] / mass_total
        return carry

    lax.fori_loop(0, N_CTX, take_grad, 0)

    def key_pair(pair, carry):
        slot_a, slot_b = 2 * pair, 2 * pair + 1
        keys = ikbuf[pl.ds(slot_a, 2)].reshape(2 * KEYS, DI)
        gkt[...] = jnp.zeros_like(gkt)

        def row_block(b, carry):
            first = pl.multiple_of(b * BLOCK, BLOCK)
            pieces = []
            for u in range(BLOCK // HI):
                t = b * (BLOCK // HI) + u
                at = pl.multiple_of(first + u * HI, HI)
                weight = rw_ref[t]
                grad_a = lg[slot_a, pl.ds(t, 1), :] * weight
                grad_b = lg[slot_b, pl.ds(t, 1), :] * weight
                heads = wb[pl.ds(at, HI), :]
                soft_a = nsp[slot_a, pl.ds(at, HI), :]
                soft_b = nsp[slot_b, pl.ds(at, HI), :]
                lanes = pl.ds(pl.multiple_of(FLAT + at, HI), HI)
                nb[lanes, :] += grad_a * soft_a + grad_b * soft_b
                part_a = (grad_a * inv_root * heads) * (1.0 - jnp.exp2(soft_a))
                part_b = (grad_b * inv_root * heads) * (1.0 - jnp.exp2(soft_b))
                pieces.append(
                    jnp.concatenate(
                        [part_a.astype(jnp.bfloat16), part_b.astype(jnp.bfloat16)], axis=1
                    )
                )
            score_grad = jnp.concatenate(pieces, axis=0)
            nb[pl.ds(first, BLOCK), :] += jnp.dot(
                score_grad, keys, preferred_element_type=jnp.float32
            )
            gkt[...] += jnp.dot(
                iqt[:, pl.ds(first, BLOCK)], score_grad, preferred_element_type=jnp.float32
            )
            return carry

        lax.fori_loop(0, FLAT // BLOCK, row_block, 0, unroll=FLAT // BLOCK)
        for part, slot in ((0, slot_a), (1, slot_b)):
            turned = gkt[:, part * KEYS : (part + 1) * KEYS].T.reshape(2, 4, 16, DI)
            gkst[slot] = turned

            def send(slot=slot):
                for i in range(4):
                    pltpu.make_async_remote_copy(
                        src_ref=gkst.at[slot, :, i],
                        dst_ref=grk.at[slot, :, i],
                        send_sem=gsend,
                        recv_sem=gsem,
                        device_id={"ctx": source(i, slot)},
                        device_id_type=MESH,
                    ).start()

            if part == 0:
                pl.when(pair > 0)(send)
            else:
                send()
        return carry

    lax.fori_loop(0, N_CTX // 2, key_pair, 0)
    out_copy = pltpu.make_async_copy(nb.at[pl.ds(0, FLAT)], gq_hbm, osem)
    out_copy.start()

    def finish_weights(r, carry):
        block = nb[pl.ds(pl.multiple_of(FLAT + r * 128, 128), 128), :]
        row = jnp.sum(block.T, axis=0, keepdims=True) * -LN2
        gw_ref[pl.ds(2 * r, 1), :] = row[:, :HI]
        gw_ref[pl.ds(2 * r + 1, 1), :] = row[:, HI:]
        return carry

    lax.fori_loop(0, FLAT // 128, finish_weights, 0)

    came = grk.at[pl.ds(1, N_CTX - 1)]
    pltpu.make_async_copy(came, came, gsem).wait()
    own_sum = gkst[0]
    for slot in range(1, N_CTX):
        own_sum = own_sum + grk[slot]
    fst[...] = own_sum.reshape(N_TP, 16, DI)
    for d in range(1, N_TP):
        peer = rem(tp + d, N_TP)
        pltpu.make_async_remote_copy(
            src_ref=fst.at[peer],
            dst_ref=frecv.at[d],
            send_sem=fsend,
            recv_sem=fsem,
            device_id={"tp": peer},
            device_id_type=MESH,
        ).start()
    landed = frecv.at[pl.ds(1, N_TP - 1)]
    pltpu.make_async_copy(landed, landed, fsem).wait()
    total = fst[tp]
    for d in range(1, N_TP):
        total = total + frecv[d]
    gk_ref[...] = total

    out_copy.wait()
    pltpu.make_async_copy(landed, landed, fsend).wait()
    sent = kbuf.at[pl.ds(0, N_CTX - 1)]
    pltpu.make_async_copy(sent, sent, ksend).wait()
    sent = ikbuf.at[pl.ds(0, N_CTX - 1)]
    pltpu.make_async_copy(sent, sent, isend).wait()
    pltpu.make_async_copy(came, came, gsend).wait()
    wait_mass_sent(0)
    wait_mass_sent(1)


def hand_over(gq_in, gw_in, gk_in, gq_out, gw_out, gk_out, gq, gw, gk, in_sems, out_sems):
    rows = FLAT // PIECES
    pieces = [pl.ds(i * rows, rows) for i in range(PIECES)]
    steps = [(gq_in.at[p], gq.at[p], gq_out.at[p]) for p in pieces]
    steps += [(gw_in, gw, gw_out), (gk_in, gk, gk_out)]
    taken = [pltpu.make_async_copy(a, b, in_sems.at[n]) for n, (a, b, c) in enumerate(steps)]
    given = [pltpu.make_async_copy(b, c, out_sems.at[n]) for n, (a, b, c) in enumerate(steps)]
    for copy in taken:
        copy.start()
    for arrival, copy in zip(taken, given):
        arrival.wait()
        copy.start()
    for copy in given:
        copy.wait()


def per_device(main_q, main_k, log_norms, index_q, index_w, index_k, row_weight, offsets, key_map):
    anywhere = pl.BlockSpec(memory_space=pl.ANY)
    vmem = pl.BlockSpec(memory_space=pltpu.VMEM)
    smem = pl.BlockSpec(memory_space=pltpu.SMEM)
    f32, bf16 = jnp.float32, jnp.bfloat16
    dma = pltpu.SemaphoreType.DMA
    grad_q, grad_w, grad_k = pl.pallas_call(
        kernel,
        out_shape=(
            jax.ShapeDtypeStruct((FLAT, DI), f32),
            jax.ShapeDtypeStruct((OWN, HI), f32),
            jax.ShapeDtypeStruct((16, DI), f32),
        ),
        in_specs=[anywhere, anywhere, anywhere, anywhere, vmem, anywhere, smem, smem, smem],
        out_specs=(anywhere, vmem, vmem),
        scratch_shapes=[
            pltpu.VMEM((HEADS, ROWS, WIDE), bf16),
            pltpu.VMEM((N_CTX, 2, 4, 16, HEADS * DQK), bf16),
            pltpu.VMEM((N_CTX, 2, 4, 16, DI), bf16),
            pltpu.VMEM((FLAT, DI), bf16),
            pltpu.VMEM((DI, FLAT), bf16),
            pltpu.VMEM((HEADS, ROWS), f32),
            pltpu.VMEM((HEADS * ROWS, 128), f32),
            pltpu.VMEM((FLAT, 128), f32),
            pltpu.VMEM((N_CTX, FLAT, 128), f32),
            pltpu.VMEM((N_CTX, OWN, 128), f32),
            pltpu.VMEM((2, ROWS, 128), f32),
            pltpu.VMEM((N_TP, N_CTX, OWN, 128), f32),
            pltpu.VMEM((DI, 2 * KEYS), f32),
            pltpu.VMEM((N_CTX, 2, 4, 16, DI), f32),
            pltpu.VMEM((N_CTX, 2, 4, 16, DI), f32),
            pltpu.VMEM((N_TP, 16, DI), f32),
            pltpu.VMEM((N_TP, 16, DI), f32),
            dma((4,)),
            dma((HEADS,)),
            dma,
            dma,
            dma((N_CTX, 2)),
            dma((N_CTX,)),
            dma((2,)),
            dma,
            dma,
            dma,
            dma,
            dma,
            dma,
        ],
        compiler_params=pltpu.CompilerParams(
            collective_id=0, has_side_effects=True, vmem_limit_bytes=VMEM_LIMIT
        ),
        name="indexer_grads",
    )(
        main_q,
        main_k.reshape(2, 4, 16, HEADS * DQK),
        log_norms.T,
        index_q.reshape(FLAT, DI),
        index_w,
        index_k.reshape(2, 4, 16, DI),
        row_weight,
        offsets,
        key_map,
    )
    grad_q, grad_w, grad_k = pl.pallas_call(
        hand_over,
        out_shape=(
            jax.ShapeDtypeStruct((FLAT, DI), f32),
            jax.ShapeDtypeStruct((OWN, HI), f32),
            jax.ShapeDtypeStruct((16, DI), f32),
        ),
        in_specs=[anywhere] * 3,
        out_specs=(anywhere,) * 3,
        scratch_shapes=[
            pltpu.VMEM((FLAT, DI), f32),
            pltpu.VMEM((OWN, HI), f32),
            pltpu.VMEM((16, DI), f32),
            dma((PIECES + 2,)),
            dma((PIECES + 2,)),
        ],
        name="hand_over",
    )(grad_q, grad_w, grad_k)
    return grad_q.reshape(OWN, HI, DI), grad_w, grad_k


def solution(mesh):
    placed = (
        P("ctx", "tp"),
        P("ctx", "tp"),
        P("ctx", "tp"),
        P(("ctx", "tp"), None, None),
        P(("ctx", "tp"), None),
        P("ctx", None),
        P(("ctx", "tp")),
        P("ctx"),
        P(),
    )
    return jax.shard_map(
        per_device,
        mesh=mesh,
        in_specs=placed,
        out_specs=(P(("ctx", "tp"), None, None), P(("ctx", "tp"), None), P(("ctx", "tp"), None)),
        check_vma=False,
    )
```

```python
import math

import jax
import jax.numpy as jnp
from jax import lax
from jax.experimental import pallas as pl
from jax.experimental.pallas import tpu as pltpu
from jax.sharding import PartitionSpec as P

MESH = pl.DeviceIdType.MESH
SIDE = 4
N_CTX = SIDE * SIDE
N_TP = 8
ROWS = 448
KEYS = 128
DQK = 192
HEADS = 16
OWN = 56
HI = 64
DI = 128
FLAT = OWN * HI
WIDE = 256
BLOCK = 512
PIECES = 4
SLOTS = 8
LAST = 24
GUEST_A = 16
GUEST_B = 21
TASKS_OWN = (2, 3, 4, 5, 8, 9, 12, 13, 14, 15, 16, 17, 20, 21, 24, 24)
TASKS_GUEST_A = (16, 17, 17, 18, 18, 19, 20, 24)
TASKS_GUEST_B = (21, 21, 21, 22, 22, 22, 22, 24)
TASKS_FIRST = (4, 5, 6, 6, 7, 7, 8, 9, 10, 10, 11, 11, 12, 13, 14, 15)
LOG2E = math.log2(math.e)
LN2 = math.log(2.0)
VMEM_LIMIT = 67043328
CONTRACT_LAST = (((1,), (1,)), ((), ()))


def rem(a, b):
    return lax.rem(a, jnp.int32(b))


def div(a, b):
    return lax.div(a, jnp.int32(b))


def at_least(i, thresholds):
    count = jnp.int32(0)
    for t in thresholds:
        count = count + (i >= t).astype(jnp.int32)
    return count


def kernel(
    q_hbm, k_hbm, norm_hbm, iq_hbm, iw_ref, ik_hbm, rw_ref, off_ref, map_ref,
    gq_hbm, gw_ref, gk_ref,
    qbuf, kbuf, relay, ikn, iq, iqt, norm, nb, wb, nsp, lg, mass, mrecv, mguest, mside, gkt, grk, fst, frecv,
    lsem, yrecv, xrecv, orecv, qrecv, nrecv, irecv, mrsem, mgsem, mssem, gsem, fsem,
    ksend, rsend, qsend, nsend, isend, msend, mssend, gsend, fsend, osem,
):
    ctx, tp = lax.axis_index("ctx"), lax.axis_index("tp")
    x, y = div(ctx, SIDE), rem(ctx, SIDE)
    side = 1 - 2 * div(tp, N_TP // 2)

    def column(dx, dy):
        return SIDE * rem(x + dx + 2 * SIDE, SIDE) + rem(y + dy + 2 * SIDE, SIDE)

    up, down, right, left = column(0, 1), column(0, -1), column(1, 0), column(-1, 0)

    def source(slot, half):
        other, opposite, hops = div(slot, SLOTS), div(rem(slot, SLOTS), SIDE), rem(slot, SIDE)
        return column(2 * opposite - other * side, hops * (1 if half else -1))

    def remote(src, dst, send, recv, **where):
        return pltpu.make_async_remote_copy(
            src_ref=src, dst_ref=dst, send_sem=send, recv_sem=recv, device_id=where,
            device_id_type=MESH,
        )

    def wait_for(ref, sem):
        pltpu.make_async_copy(ref, ref, sem).wait()

    local = [
        pltpu.make_async_copy(k_hbm, kbuf.at[0], lsem.at[0]),
        pltpu.make_async_copy(ik_hbm.at[tp], ikn.at[ctx, tp], lsem.at[1]),
        pltpu.make_async_copy(norm_hbm, norm.at[2], lsem.at[2]),
        pltpu.make_async_copy(q_hbm, qbuf.at[0], lsem.at[3]),
        pltpu.make_async_copy(iq_hbm, iq, lsem.at[4]),
    ]
    for copy in local:
        copy.start()
    barrier = pltpu.get_barrier_semaphore()
    for d in range(1, SIDE):
        for peer in (column(d, 0), column(0, d)):
            pl.semaphore_signal(barrier, inc=1, device_id={"ctx": peer}, device_id_type=MESH)
    for d in range(1, N_TP):
        pl.semaphore_signal(
            barrier, inc=1, device_id={"tp": rem(tp + d, N_TP)}, device_id_type=MESH
        )
    pl.semaphore_wait(barrier, 2 * (SIDE - 1) + N_TP - 1)

    def send_y(slot, k):
        for half, peer in ((0, up), (1, down)):
            remote(
                kbuf.at[slot, half, k], kbuf.at[slot + 1, half, k], ksend, yrecv.at[slot + 1, k],
                ctx=peer,
            ).start()

    local[0].wait()
    for k in range(4):
        for half, peer in ((0, right), (1, left)):
            remote(
                kbuf.at[0, half, k], relay.at[half, k], rsend, xrecv.at[k], ctx=peer
            ).start()
        send_y(0, k)
    local[1].wait()
    for d in range(1, SIDE):
        remote(
            ikn.at[ctx, tp], ikn.at[ctx, tp], isend.at[0], irecv.at[0], ctx=column(0, d)
        ).start()
    local[2].wait()
    remote(norm.at[2], norm.at[0], nsend, nrecv, ctx=left).start()
    remote(norm.at[2], norm.at[1], nsend, nrecv, ctx=right).start()

    def spread_norms(kind, values):
        turned = values.T * LOG2E
        for head in range(HEADS):
            nb[kind, head * ROWS : (head + 1) * ROWS, :] = jnp.broadcast_to(
                turned[:, head : head + 1], (ROWS, 128)
            )

    spread_norms(0, norm[2])
    own_x = pl.ds(SIDE * x, SIDE)
    wait_for(ikn.at[pl.ds(0, SIDE - 1), 0], irecv.at[0])
    for d in range(1, SIDE):
        remote(
            ikn.at[own_x, tp], ikn.at[own_x, tp], isend.at[1], irecv.at[1], ctx=column(d, 0)
        ).start()
    weights_down = iw_ref[...].T
    for t in range(OWN):
        wb[t * HI : (t + 1) * HI, :] = jnp.broadcast_to(weights_down[:, t : t + 1], (HI, 128))
    wait_for(ikn.at[pl.ds(0, N_CTX - SIDE), 0], irecv.at[1])
    for d in range(1, N_TP):
        remote(
            ikn.at[:, tp], ikn.at[:, tp], isend.at[2], irecv.at[2], tp=rem(tp + d, N_TP)
        ).start()
    local[3].wait()
    local[4].wait()

    def turn_queries(b, carry):
        first = pl.multiple_of(b * WIDE, WIDE)
        iqt[:, pl.ds(first, WIDE)] = iq[pl.ds(first, WIDE), :].astype(jnp.float32).T.astype(jnp.bfloat16)
        return carry

    score_scale = LOG2E / math.sqrt(DQK)
    inv_root = 1.0 / math.sqrt(DI)
    quarter = ROWS // 4
    low = lax.broadcasted_iota(jnp.int32, (KEYS, 128), 1) < 64
    low = jnp.where(low, 1.0, 0.0).astype(jnp.bfloat16)
    high = (1.0 - low.astype(jnp.float32)).astype(jnp.bfloat16)

    def head_mass(kind, slot, part):
        firsts = [
            pl.multiple_of(part * quarter, 16),
            pl.multiple_of(part * quarter + ROWS // 2, 16),
        ]
        total = None
        for pair in range(HEADS // 2):
            base = pair * 2 * DQK
            tiles = [
                kbuf[slot, :, :, :, base + 128 * j : base + 128 * (j + 1)].reshape(KEYS, 128)
                for j in range(3)
            ]
            keys = [
                jnp.concatenate([tiles[0], tiles[1] * low], axis=1),
                jnp.concatenate([tiles[1] * high, tiles[2]], axis=1),
            ]
            for u in range(2):
                col = base + 128 * u
                queries = jnp.concatenate(
                    [qbuf[kind, pl.ds(f, quarter), col : col + WIDE] for f in firsts], axis=0
                )
                at = (2 * pair + u) * ROWS
                norms = jnp.concatenate(
                    [nb[kind, pl.ds(pl.multiple_of(at + f, 16), quarter), :] for f in firsts], axis=0
                )
                scores = lax.dot_general(
                    queries, keys[u], CONTRACT_LAST, preferred_element_type=jnp.float32
                )
                term = jnp.exp2(scores * score_scale - norms)
                total = term if total is None else total + term
        number = (kind * SLOTS + slot) * 2 + part
        mass[number] = total.reshape(4, OWN, 128)
        for j in range(4):
            peer = 2 * part + j % 2 + 4 * (j // 2)
            away = rem(tp - peer + N_TP, N_TP)
            if kind:
                landing, recv = mguest.at[away, slot], mgsem.at[div(slot, SLOTS - 1)]
            else:
                landing, recv = mrecv.at[away, slot], mrsem

            @pl.when(peer != tp)
            def _():
                remote(mass.at[number, j], landing, msend, recv, tp=peer).start()

            @pl.when(peer == tp)
            def _():
                landing[...] = mass[number, j]

    def first_pass(slot):
        keys = jnp.concatenate(
            [
                ikn[source(slot, 0), 0:4].reshape(KEYS // 2, DI),
                ikn[source(slot, 1), 4:8].reshape(KEYS // 2, DI),
            ],
            axis=0,
        )

        def eight_rows(b, carry):
            rows = []
            for part in range(2):
                first = pl.multiple_of(b * 8 * HI + part * 4 * HI, 4 * HI)
                inner = lax.dot_general(
                    iq[pl.ds(first, 4 * HI), :], keys, CONTRACT_LAST,
                    preferred_element_type=jnp.float32,
                )
                v = inner * (inv_root * LOG2E)
                minus = jnp.minimum(-v, 0.0) - jnp.log2(1.0 + jnp.exp2(-jnp.abs(v)))
                nsp[slot, pl.ds(first, 4 * HI), :] = minus
                weighted = wb[pl.ds(first, 4 * HI), :] * minus
                for u in range(4):
                    rows.append(
                        jnp.sum(weighted[u * HI : (u + 1) * HI, :], axis=0, keepdims=True)
                    )
            lg[slot, pl.ds(pl.multiple_of(b * 8, 8), 8), :] = jnp.concatenate(rows, axis=0)
            return carry

        lax.fori_loop(0, OWN // 8, eight_rows, 0, unroll=7)

    def add_guests(slot):
        amount = mguest[0, slot]
        for d in range(1, N_TP):
            amount = amount + mguest[d, slot]
        mguest[0, slot] = amount

    def run_tasks(i, thresholds, task):
        def one(m, carry):
            task(m)
            return carry

        lax.fori_loop(at_least(i - 1, thresholds), at_least(i, thresholds), one, 0)

    def step(i, carry):
        k = rem(i, 4)

        @pl.when(i < LAST)
        def _():
            slot = SIDE * div(i, LAST // 2) + div(rem(i, LAST // 2), 4) + 1
            wait_for(kbuf.at[slot, :, k], yrecv.at[slot, k])

            @pl.when(rem(slot, SIDE) < SIDE - 1)
            def _():
                send_y(slot, k)

        @pl.when(i < 4)
        def _():
            wait_for(relay.at[:, k], xrecv.at[k])
            for half, peer in ((0, right), (1, left)):
                remote(
                    relay.at[half, k], kbuf.at[SIDE, half, k], rsend, orecv.at[k], ctx=peer
                ).start()

        @pl.when(i == 3)
        def _():
            for part in range(2):
                for first, peer in ((0, left), (ROWS // 2, right)):
                    rows = pl.ds(first + part * quarter, quarter)
                    remote(
                        qbuf.at[0, rows], qbuf.at[1, rows], qsend, qrecv.at[part], ctx=peer
                    ).start()

        @pl.when((i >= 8) & (i < 12))
        def _():
            wait_for(kbuf.at[SIDE, :, k], orecv.at[k])
            send_y(SIDE, k)

        @pl.when(i == 3)
        def _():
            lax.fori_loop(0, FLAT // WIDE, turn_queries, 0)

        @pl.when(i == 4)
        def _():
            wait_for(ikn.at[:, pl.ds(0, N_TP - 1)], irecv.at[2])

        @pl.when(i == GUEST_A)
        def _():
            wait_for(norm.at[pl.ds(0, 2)], nrecv)
            nearer = lax.broadcasted_iota(jnp.int32, (HEADS, ROWS), 1) < ROWS // 2
            spread_norms(1, jnp.where(nearer, norm[0], norm[1]))
            wait_for(qbuf.at[1, pl.ds(0, 2 * quarter)], qrecv.at[0])

        @pl.when(i == GUEST_B)
        def _():
            wait_for(qbuf.at[1, pl.ds(0, 2 * quarter)], qrecv.at[1])

        @pl.when(i == LAST)
        def _():
            wait_for(mguest.at[pl.ds(1, N_TP - 1), pl.ds(0, SLOTS - 1)], mgsem.at[0])
            for slot in range(SLOTS - 1):
                add_guests(slot)
            early = pl.ds(0, SLOTS - 1)
            remote(
                mguest.at[0, early], mside.at[early], mssend, mssem.at[0], ctx=column(side, 0)
            ).start()

        run_tasks(i, TASKS_GUEST_A, lambda m: head_mass(1, m, 0))
        run_tasks(i, TASKS_GUEST_B, lambda m: head_mass(1, m, 1))
        run_tasks(i, TASKS_OWN, lambda m: head_mass(0, div(m, 2), rem(m, 2)))
        run_tasks(i, TASKS_FIRST, first_pass)
        return carry

    lax.fori_loop(0, LAST + 1, step, 0)
    nb[0] = jnp.zeros_like(nb[0])
    wait_for(mguest.at[pl.ds(1, N_TP - 1), SLOTS - 1], mgsem.at[1])
    add_guests(SLOTS - 1)
    remote(
        mguest.at[0, SLOTS - 1], mside.at[SLOTS - 1], mssend, mssem.at[1], ctx=column(side, 0)
    ).start()

    lane = lax.broadcasted_iota(jnp.int32, (OWN, 128), 1)
    row_pos = off_ref[0] + tp * OWN + lax.broadcasted_iota(jnp.int32, (OWN, 128), 0)

    def visible_at(slot):
        block = jnp.where(
            lane < 64, map_ref[source(slot, 0)] * KEYS, map_ref[source(slot, 1)] * KEYS
        )
        return block + lane <= row_pos

    def take_max(slot, top):
        masked = jnp.where(visible_at(slot), -lg[slot], -jnp.inf)
        lg[slot] = masked
        return jnp.maximum(top, masked)

    top = lax.fori_loop(0, N_CTX, take_max, jnp.full((OWN, 128), -jnp.inf, jnp.float32))
    top = jnp.max(top, axis=1, keepdims=True)

    def take_exp(slot, total):
        term = jnp.exp2(lg[slot] - top)
        lg[slot] = term
        return total + term

    exp_total = lax.fori_loop(0, N_CTX, take_exp, jnp.zeros((OWN, 128), jnp.float32))
    exp_share = 1.0 / jnp.sum(exp_total, axis=1, keepdims=True)

    wait_for(mrecv.at[pl.ds(1, N_TP - 1)], mrsem)

    def add_own(slot, total):
        amount = mrecv[0, slot]
        for d in range(1, N_TP):
            amount = amount + mrecv[d, slot]
        amount = jnp.where(visible_at(slot), amount, 0.0)
        mrecv[0, slot] = amount
        return total + amount

    def add_side(slot, total):
        amount = jnp.where(visible_at(SLOTS + slot), mside[slot], 0.0)
        mrecv[1, slot] = amount
        return total + amount

    mass_total = lax.fori_loop(0, SLOTS, add_own, jnp.zeros((OWN, 128), jnp.float32))
    wait_for(mside.at[pl.ds(0, SLOTS - 1)], mssem.at[0])
    wait_for(mside.at[SLOTS - 1], mssem.at[1])
    mass_total = lax.fori_loop(0, SLOTS, add_side, mass_total)
    mass_total = jnp.sum(mass_total, axis=1, keepdims=True)

    def take_grad(slot, carry):
        amount = mrecv[div(slot, SLOTS), rem(slot, SLOTS)]
        lg[slot] = lg[slot] * exp_share - amount / mass_total
        return carry

    lax.fori_loop(0, N_CTX, take_grad, 0)

    def key_pair(pair, carry):
        slot_a, slot_b = 2 * pair, 2 * pair + 1
        keys = jnp.concatenate(
            [
                ikn[source(slot, half), 4 * half : 4 * half + 4].reshape(KEYS // 2, DI)
                for slot in (slot_a, slot_b)
                for half in range(2)
            ],
            axis=0,
        )
        gkt[...] = jnp.zeros_like(gkt)

        def row_block(b, carry):
            first = pl.multiple_of(b * BLOCK, BLOCK)
            pieces = []
            for u in range(BLOCK // HI):
                t = b * (BLOCK // HI) + u
                at = pl.multiple_of(first + u * HI, HI)
                weight = rw_ref[t]
                grad_a = lg[slot_a, pl.ds(t, 1), :] * weight
                grad_b = lg[slot_b, pl.ds(t, 1), :] * weight
                heads = wb[pl.ds(at, HI), :]
                soft_a = nsp[slot_a, pl.ds(at, HI), :]
                soft_b = nsp[slot_b, pl.ds(at, HI), :]
                lanes = pl.ds(pl.multiple_of(FLAT + at, HI), HI)
                nb[0, lanes, :] += grad_a * soft_a + grad_b * soft_b
                part_a = (grad_a * inv_root * heads) * (1.0 - jnp.exp2(soft_a))
                part_b = (grad_b * inv_root * heads) * (1.0 - jnp.exp2(soft_b))
                pieces.append(
                    jnp.concatenate(
                        [part_a.astype(jnp.bfloat16), part_b.astype(jnp.bfloat16)], axis=1
                    )
                )
            score_grad = jnp.concatenate(pieces, axis=0)
            nb[0, pl.ds(first, BLOCK), :] += jnp.dot(
                score_grad, keys, preferred_element_type=jnp.float32
            )
            gkt[...] += jnp.dot(
                iqt[:, pl.ds(first, BLOCK)], score_grad, preferred_element_type=jnp.float32
            )
            return carry

        lax.fori_loop(0, FLAT // BLOCK, row_block, 0, unroll=FLAT // BLOCK)
        at = pl.multiple_of(pair * 2 * KEYS, 2 * KEYS)
        nb[1, pl.ds(at, 2 * KEYS), :] = gkt[...].T
        for part, slot in ((0, slot_a), (1, slot_b)):

            def send(part=part, slot=slot):
                for half in range(2):
                    rows = pl.ds(pl.multiple_of(at + part * KEYS + half * 64, 64), 64)
                    remote(
                        nb.at[1, rows], grk.at[rows], gsend, gsem, ctx=source(slot, half)
                    ).start()

            if part == 0:
                pl.when(pair > 0)(send)
            else:
                send()
        return carry

    lax.fori_loop(0, N_CTX // 2, key_pair, 0)
    out_copy = pltpu.make_async_copy(nb.at[0, pl.ds(0, FLAT)], gq_hbm, osem)
    out_copy.start()

    def finish_weights(r, carry):
        block = nb[0, pl.ds(pl.multiple_of(FLAT + r * 128, 128), 128), :]
        row = jnp.sum(block.T, axis=0, keepdims=True) * -LN2
        gw_ref[pl.ds(2 * r, 1), :] = row[:, :HI]
        gw_ref[pl.ds(2 * r + 1, 1), :] = row[:, HI:]
        return carry

    lax.fori_loop(0, FLAT // 128, finish_weights, 0)

    came = grk.at[pl.ds(KEYS, (N_CTX - 1) * KEYS)]
    wait_for(came, gsem)
    own_sum = nb[1, 0:KEYS, :]
    for slot in range(1, N_CTX):
        own_sum = own_sum + grk[slot * KEYS : (slot + 1) * KEYS, :]
    fst[...] = own_sum.reshape(N_TP, 16, DI)
    for d in range(1, N_TP):
        peer = rem(tp + d, N_TP)
        remote(fst.at[peer], frecv.at[d], fsend, fsem, tp=peer).start()
    landed = frecv.at[pl.ds(1, N_TP - 1)]
    wait_for(landed, fsem)
    total = fst[tp]
    for d in range(1, N_TP):
        total = total + frecv[d]
    gk_ref[...] = total

    out_copy.wait()
    wait_for(landed, fsend)
    wait_for(came, gsend)
    wait_for(kbuf.at[pl.ds(0, SLOTS - 2)], ksend)
    wait_for(kbuf.at[pl.ds(0, 2)], rsend)
    wait_for(qbuf.at[1], qsend)
    wait_for(norm.at[pl.ds(0, 2)], nsend)
    wait_for(ikn.at[pl.ds(0, SIDE - 1), 0], isend.at[0])
    wait_for(ikn.at[pl.ds(0, N_CTX - SIDE), 0], isend.at[1])
    wait_for(ikn.at[:, pl.ds(0, N_TP - 1)], isend.at[2])
    wait_for(mside, mssend)
    wait_for(mass.at[pl.ds(0, 4 * (N_TP - 1))], msend)


def hand_over(gq_in, gw_in, gk_in, gq_out, gw_out, gk_out, gq, gw, gk, in_sems, out_sems):
    rows = FLAT // PIECES
    pieces = [pl.ds(i * rows, rows) for i in range(PIECES)]
    steps = [(gq_in.at[p], gq.at[p], gq_out.at[p]) for p in pieces]
    steps += [(gw_in, gw, gw_out), (gk_in, gk, gk_out)]
    taken = [pltpu.make_async_copy(a, b, in_sems.at[n]) for n, (a, b, c) in enumerate(steps)]
    given = [pltpu.make_async_copy(b, c, out_sems.at[n]) for n, (a, b, c) in enumerate(steps)]
    for copy in taken:
        copy.start()
    for arrival, copy in zip(taken, given):
        arrival.wait()
        copy.start()
    for copy in given:
        copy.wait()


def per_device(main_q, main_k, log_norms, index_q, index_w, index_k, row_weight, offsets, key_map):
    anywhere = pl.BlockSpec(memory_space=pl.ANY)
    vmem = pl.BlockSpec(memory_space=pltpu.VMEM)
    smem = pl.BlockSpec(memory_space=pltpu.SMEM)
    f32, bf16 = jnp.float32, jnp.bfloat16
    dma = pltpu.SemaphoreType.DMA
    grad_q, grad_w, grad_k = pl.pallas_call(
        kernel,
        out_shape=(
            jax.ShapeDtypeStruct((FLAT, DI), f32),
            jax.ShapeDtypeStruct((OWN, HI), f32),
            jax.ShapeDtypeStruct((16, DI), f32),
        ),
        in_specs=[anywhere, anywhere, anywhere, anywhere, vmem, anywhere, smem, smem, smem],
        out_specs=(anywhere, vmem, vmem),
        scratch_shapes=[
            pltpu.VMEM((2, ROWS, HEADS * DQK), bf16),
            pltpu.VMEM((SLOTS, 2, 4, 16, HEADS * DQK), bf16),
            pltpu.VMEM((2, 4, 16, HEADS * DQK), bf16),
            pltpu.VMEM((N_CTX, N_TP, 16, DI), bf16),
            pltpu.VMEM((FLAT, DI), bf16),
            pltpu.VMEM((DI, FLAT), bf16),
            pltpu.VMEM((3, HEADS, ROWS), f32),
            pltpu.VMEM((2, HEADS * ROWS, 128), f32),
            pltpu.VMEM((FLAT, 128), f32),
            pltpu.VMEM((N_CTX, FLAT, 128), f32),
            pltpu.VMEM((N_CTX, OWN, 128), f32),
            pltpu.VMEM((4 * SLOTS, 4, OWN, 128), f32),
            pltpu.VMEM((N_TP, SLOTS, OWN, 128), f32),
            pltpu.VMEM((N_TP, SLOTS, OWN, 128), f32),
            pltpu.VMEM((SLOTS, OWN, 128), f32),
            pltpu.VMEM((DI, 2 * KEYS), f32),
            pltpu.VMEM((N_CTX * KEYS, DI), f32),
            pltpu.VMEM((N_TP, 16, DI), f32),
            pltpu.VMEM((N_TP, 16, DI), f32),
            dma((5,)),
            dma((SLOTS, 4)),
            dma((4,)),
            dma((4,)),
            dma((2,)),
            dma,
            dma((3,)),
            dma,
            dma((2,)),
            dma((2,)),
            dma,
            dma,
            dma,
            dma,
            dma,
            dma,
            dma((3,)),
            dma,
            dma,
            dma,
            dma,
            dma,
        ],
        compiler_params=pltpu.CompilerParams(
            collective_id=0, has_side_effects=True, vmem_limit_bytes=VMEM_LIMIT
        ),
        name="indexer_grads",
    )(
        main_q,
        main_k.reshape(2, 4, 16, HEADS * DQK),
        log_norms.T,
        index_q.reshape(FLAT, DI),
        index_w,
        index_k.reshape(N_TP, 16, DI),
        row_weight,
        offsets,
        key_map,
    )
    grad_q, grad_w, grad_k = pl.pallas_call(
        hand_over,
        out_shape=(
            jax.ShapeDtypeStruct((FLAT, DI), f32),
            jax.ShapeDtypeStruct((OWN, HI), f32),
            jax.ShapeDtypeStruct((16, DI), f32),
        ),
        in_specs=[anywhere] * 3,
        out_specs=(anywhere,) * 3,
        scratch_shapes=[
            pltpu.VMEM((FLAT, DI), f32),
            pltpu.VMEM((OWN, HI), f32),
            pltpu.VMEM((16, DI), f32),
            dma((PIECES + 2,)),
            dma((PIECES + 2,)),
        ],
        name="hand_over",
    )(grad_q, grad_w, grad_k)
    return grad_q.reshape(OWN, HI, DI), grad_w, grad_k


def solution(mesh):
    placed = (
        P("ctx", "tp"),
        P("ctx", "tp"),
        P("ctx", "tp"),
        P(("ctx", "tp"), None, None),
        P(("ctx", "tp"), None),
        P("ctx", None),
        P(("ctx", "tp")),
        P("ctx"),
        P(),
    )
    return jax.shard_map(
        per_device,
        mesh=mesh,
        in_specs=placed,
        out_specs=(P(("ctx", "tp"), None, None), P(("ctx", "tp"), None), P(("ctx", "tp"), None)),
        check_vma=False,
    )
```

```python
import math

import jax
import jax.numpy as jnp
from jax import lax
from jax.experimental import pallas as pl
from jax.experimental.pallas import tpu as pltpu
from jax.sharding import PartitionSpec as P

MESH = pl.DeviceIdType.MESH
SIDE = 4
N_CTX = SIDE * SIDE
N_TP = 8
ROWS = 448
KEYS = 128
DQK = 192
HEADS = 16
OWN = 56
HI = 64
DI = 128
FLAT = OWN * HI
WIDE = 256
BLOCK = 512
PIECES = 4
SLOTS = 8
LAST = 24
EARLY = 4
GUEST_A = 16
GUEST_B = 21
TASKS_OWN = (2, 3, 4, 5, 8, 9, 12, 13, 14, 15, 16, 17, 20, 21, 24, 24)
TASKS_GUEST_A = (16, 17, 17, 18, 18, 19, 20, 24)
TASKS_GUEST_B = (21, 21, 21, 21, 22, 22, 22, 24)
TASKS_FIRST = (4, 5, 6, 6, 7, 7, 8, 9, 10, 10, 11, 11, 12, 13, 14, 15)
LOG2E = math.log2(math.e)
LN2 = math.log(2.0)
VMEM_LIMIT = 67043328
CONTRACT_LAST = (((1,), (1,)), ((), ()))


def rem(a, b):
    return lax.rem(a, jnp.int32(b))


def div(a, b):
    return lax.div(a, jnp.int32(b))


def at_least(i, thresholds):
    count = jnp.int32(0)
    for t in thresholds:
        count = count + (i >= t).astype(jnp.int32)
    return count


def kernel(
    q_hbm, k_hbm, norm_hbm, iq_hbm, iw_ref, ik_hbm, rw_ref, off_ref, map_ref,
    gq_hbm, gw_ref, gk_ref,
    qbuf, kbuf, relay, ikn, iq, iqt, norm, nb, wb, nsp, lg, mass, mrecv, mguest, gsum, mside, mlast, share, gkt, grk, fst, frecv,
    lsem, yrecv, xrecv, orecv, qrecv, nrecv, irecv, mrsem, mgsem, mssem, mlsem, gsem, fsem,
    ksend, rsend, qsend, nsend, isend, msend, dsend, mssend, gsend, fsend, osem,
):
    ctx, tp = lax.axis_index("ctx"), lax.axis_index("tp")
    x, y = div(ctx, SIDE), rem(ctx, SIDE)
    side = 1 - 2 * div(tp, N_TP // 2)

    def column(dx, dy):
        return SIDE * rem(x + dx + 2 * SIDE, SIDE) + rem(y + dy + 2 * SIDE, SIDE)

    up, down, right, left = column(0, 1), column(0, -1), column(1, 0), column(-1, 0)

    def source(slot, half):
        other, opposite, hops = div(slot, SLOTS), div(rem(slot, SLOTS), SIDE), rem(slot, SIDE)
        return column(2 * opposite - other * side, hops * (1 if half else -1))

    def remote(src, dst, send, recv, **where):
        return pltpu.make_async_remote_copy(
            src_ref=src, dst_ref=dst, send_sem=send, recv_sem=recv, device_id=where,
            device_id_type=MESH,
        )

    def wait_for(ref, sem):
        pltpu.make_async_copy(ref, ref, sem).wait()

    local = [
        pltpu.make_async_copy(k_hbm, kbuf.at[0], lsem.at[0]),
        pltpu.make_async_copy(ik_hbm.at[tp], ikn.at[ctx, tp], lsem.at[1]),
        pltpu.make_async_copy(norm_hbm, norm.at[2], lsem.at[2]),
        pltpu.make_async_copy(q_hbm, qbuf.at[0], lsem.at[3]),
        pltpu.make_async_copy(iq_hbm, iq, lsem.at[4]),
    ]
    for copy in local:
        copy.start()
    barrier = pltpu.get_barrier_semaphore()
    for d in range(1, SIDE):
        for peer in (column(d, 0), column(0, d)):
            pl.semaphore_signal(barrier, inc=1, device_id={"ctx": peer}, device_id_type=MESH)
    for d in range(1, N_TP):
        pl.semaphore_signal(
            barrier, inc=1, device_id={"tp": rem(tp + d, N_TP)}, device_id_type=MESH
        )
    pl.semaphore_wait(barrier, 2 * (SIDE - 1) + N_TP - 1)

    def send_y(slot, k):
        for half, peer in ((0, up), (1, down)):
            remote(
                kbuf.at[slot, half, k], kbuf.at[slot + 1, half, k], ksend, yrecv.at[slot + 1, k],
                ctx=peer,
            ).start()

    local[1].wait()
    for d in range(1, SIDE):
        remote(
            ikn.at[ctx, tp], ikn.at[ctx, tp], isend.at[0], irecv.at[0], ctx=column(0, d)
        ).start()
    local[0].wait()
    for k in range(4):
        send_y(0, k)
    own_x = pl.ds(SIDE * x, SIDE)
    wait_for(ikn.at[pl.ds(0, SIDE - 1), 0], irecv.at[0])
    for d in range(1, SIDE):
        remote(
            ikn.at[own_x, tp], ikn.at[own_x, tp], isend.at[1], irecv.at[1], ctx=column(d, 0)
        ).start()
    for k in range(4):
        for half, peer in ((0, right), (1, left)):
            remote(
                kbuf.at[0, half, k], relay.at[half, k], rsend, xrecv.at[k], ctx=peer
            ).start()
    local[2].wait()

    def spread_norms(kind, values):
        turned = values.T * LOG2E
        for head in range(HEADS):
            nb[kind, head * ROWS : (head + 1) * ROWS, :] = jnp.broadcast_to(
                turned[:, head : head + 1], (ROWS, 128)
            )

    spread_norms(0, norm[2])
    weights_down = iw_ref[...].T
    for t in range(OWN):
        wb[t * HI : (t + 1) * HI, :] = jnp.broadcast_to(weights_down[:, t : t + 1], (HI, 128))
    wait_for(ikn.at[pl.ds(0, N_CTX - SIDE), 0], irecv.at[1])
    for d in range(1, N_TP):
        remote(
            ikn.at[:, tp], ikn.at[:, tp], isend.at[2], irecv.at[2], tp=rem(tp + d, N_TP)
        ).start()
    local[3].wait()
    local[4].wait()

    def turn_queries(b, carry):
        first = pl.multiple_of(b * WIDE, WIDE)
        iqt[:, pl.ds(first, WIDE)] = iq[pl.ds(first, WIDE), :].astype(jnp.float32).T.astype(jnp.bfloat16)
        return carry

    score_scale = LOG2E / math.sqrt(DQK)
    inv_root = 1.0 / math.sqrt(DI)
    quarter = ROWS // 4
    low = lax.broadcasted_iota(jnp.int32, (KEYS, 128), 1) < 64
    low = jnp.where(low, 1.0, 0.0).astype(jnp.bfloat16)
    high = (1.0 - low.astype(jnp.float32)).astype(jnp.bfloat16)

    def head_mass(kind, slot, part):
        firsts = [
            pl.multiple_of(part * quarter, 16),
            pl.multiple_of(part * quarter + ROWS // 2, 16),
        ]
        total = None
        for pair in range(HEADS // 2):
            base = pair * 2 * DQK
            tiles = [
                kbuf[slot, :, :, :, base + 128 * j : base + 128 * (j + 1)].reshape(KEYS, 128)
                for j in range(3)
            ]
            keys = [
                jnp.concatenate([tiles[0], tiles[1] * low], axis=1),
                jnp.concatenate([tiles[1] * high, tiles[2]], axis=1),
            ]
            for u in range(2):
                col = base + 128 * u
                queries = jnp.concatenate(
                    [qbuf[kind, pl.ds(f, quarter), col : col + WIDE] for f in firsts], axis=0
                )
                at = (2 * pair + u) * ROWS
                norms = jnp.concatenate(
                    [nb[kind, pl.ds(pl.multiple_of(at + f, 16), quarter), :] for f in firsts], axis=0
                )
                scores = lax.dot_general(
                    queries, keys[u], CONTRACT_LAST, preferred_element_type=jnp.float32
                )
                term = jnp.exp2(scores * score_scale - norms)
                total = term if total is None else total + term
        number = (kind * SLOTS + slot) * 2 + part
        mass[number] = total.reshape(4, OWN, 128).astype(jnp.bfloat16)
        for j in range(4):
            peer = 2 * part + j % 2 + 4 * (j // 2)
            away = rem(tp - peer + N_TP, N_TP)
            if kind:
                landing, recv = mguest.at[away, slot], mgsem.at[div(slot, EARLY)]
                inside = slot < SLOTS - 1

                @pl.when(slot == SLOTS - 1)
                def _():
                    remote(
                        mass.at[number, j], mlast.at[away], dsend, mlsem,
                        ctx=column(1 - 2 * (j // 2), 0), tp=peer,
                    ).start()

            else:
                landing, recv = mrecv.at[away, slot], mrsem
                inside = slot < SLOTS

            @pl.when(inside & (peer != tp))
            def _():
                remote(mass.at[number, j], landing, msend.at[kind], recv, tp=peer).start()

            @pl.when(inside & (peer == tp))
            def _():
                landing[...] = mass[number, j]

    def first_pass(slot):
        keys = jnp.concatenate(
            [
                ikn[source(slot, 0), 0:4].reshape(KEYS // 2, DI),
                ikn[source(slot, 1), 4:8].reshape(KEYS // 2, DI),
            ],
            axis=0,
        )

        def eight_rows(b, carry):
            rows = []
            for part in range(2):
                first = pl.multiple_of(b * 8 * HI + part * 4 * HI, 4 * HI)
                inner = lax.dot_general(
                    iq[pl.ds(first, 4 * HI), :], keys, CONTRACT_LAST,
                    preferred_element_type=jnp.float32,
                )
                v = inner * (inv_root * LOG2E)
                minus = jnp.minimum(-v, 0.0) - jnp.log2(1.0 + jnp.exp2(-jnp.abs(v)))
                nsp[slot, pl.ds(first, 4 * HI), :] = minus
                weighted = wb[pl.ds(first, 4 * HI), :] * minus
                for u in range(4):
                    rows.append(
                        jnp.sum(weighted[u * HI : (u + 1) * HI, :], axis=0, keepdims=True)
                    )
            lg[slot, pl.ds(pl.multiple_of(b * 8, 8), 8), :] = jnp.concatenate(rows, axis=0)
            return carry

        lax.fori_loop(0, OWN // 8, eight_rows, 0, unroll=7)

    def pass_guests(batch):
        first, count = ((0, EARLY), (EARLY, SLOTS - 1 - EARLY))[batch]
        slots = pl.ds(first, count)
        wait_for(mguest.at[pl.ds(1, N_TP - 1), slots], mgsem.at[batch])
        for slot in range(first, first + count):
            amount = mguest[0, slot].astype(jnp.float32)
            for d in range(1, N_TP):
                amount = amount + mguest[d, slot].astype(jnp.float32)
            gsum[slot] = amount
        remote(
            gsum.at[slots], mside.at[slots], mssend, mssem.at[batch], ctx=column(side, 0)
        ).start()

    def run_tasks(i, thresholds, task):
        def one(m, carry):
            task(m)
            return carry

        lax.fori_loop(at_least(i - 1, thresholds), at_least(i, thresholds), one, 0)

    def step(i, carry):
        k = rem(i, 4)

        @pl.when(i == LAST - 1)
        def _():
            pass_guests(0)

        @pl.when(i < LAST)
        def _():
            slot = SIDE * div(i, LAST // 2) + div(rem(i, LAST // 2), 4) + 1
            wait_for(kbuf.at[slot, :, k], yrecv.at[slot, k])

            @pl.when(rem(slot, SIDE) < SIDE - 1)
            def _():
                send_y(slot, k)

        @pl.when(i < 4)
        def _():
            wait_for(relay.at[:, k], xrecv.at[k])
            for half, peer in ((0, right), (1, left)):
                remote(
                    relay.at[half, k], kbuf.at[SIDE, half, k], rsend, orecv.at[k], ctx=peer
                ).start()

        @pl.when(i == 3)
        def _():
            remote(norm.at[2], norm.at[0], nsend, nrecv, ctx=left).start()
            remote(norm.at[2], norm.at[1], nsend, nrecv, ctx=right).start()
            for part in range(2):
                for first, peer in ((0, left), (ROWS // 2, right)):
                    rows = pl.ds(first + part * quarter, quarter)
                    remote(
                        qbuf.at[0, rows], qbuf.at[1, rows], qsend, qrecv.at[part], ctx=peer
                    ).start()

        @pl.when((i >= 8) & (i < 12))
        def _():
            wait_for(kbuf.at[SIDE, :, k], orecv.at[k])
            send_y(SIDE, k)

        @pl.when(i == 3)
        def _():
            lax.fori_loop(0, FLAT // WIDE, turn_queries, 0)

        @pl.when(i == 4)
        def _():
            wait_for(ikn.at[:, pl.ds(0, N_TP - 1)], irecv.at[2])

        @pl.when(i == GUEST_A)
        def _():
            wait_for(norm.at[pl.ds(0, 2)], nrecv)
            nearer = lax.broadcasted_iota(jnp.int32, (HEADS, ROWS), 1) < ROWS // 2
            spread_norms(1, jnp.where(nearer, norm[0], norm[1]))
            wait_for(qbuf.at[1, pl.ds(0, 2 * quarter)], qrecv.at[0])

        @pl.when(i == GUEST_B)
        def _():
            wait_for(qbuf.at[1, pl.ds(0, 2 * quarter)], qrecv.at[1])

        @pl.when(i == LAST)
        def _():
            pass_guests(1)

        run_tasks(i, TASKS_GUEST_A, lambda m: head_mass(1, m, 0))
        run_tasks(i, TASKS_GUEST_B, lambda m: head_mass(1, m, 1))
        run_tasks(i, TASKS_OWN, lambda m: head_mass(0, div(m, 2), rem(m, 2)))
        run_tasks(i, TASKS_FIRST, first_pass)
        return carry

    lax.fori_loop(0, LAST + 1, step, 0)
    nb[0] = jnp.zeros_like(nb[0])
    lane = lax.broadcasted_iota(jnp.int32, (OWN, 128), 1)
    row_pos = off_ref[0] + tp * OWN + lax.broadcasted_iota(jnp.int32, (OWN, 128), 0)

    def visible_at(slot):
        block = jnp.where(
            lane < 64, map_ref[source(slot, 0)] * KEYS, map_ref[source(slot, 1)] * KEYS
        )
        return block + lane <= row_pos

    def take_max(slot, top):
        masked = jnp.where(visible_at(slot), -lg[slot], -jnp.inf)
        lg[slot] = masked
        return jnp.maximum(top, masked)

    top = lax.fori_loop(0, N_CTX, take_max, jnp.full((OWN, 128), -jnp.inf, jnp.float32))
    top = jnp.max(top, axis=1, keepdims=True)

    def take_exp(slot, total):
        term = jnp.exp2(lg[slot] - top)
        lg[slot] = term
        return total + term

    exp_total = lax.fori_loop(0, N_CTX, take_exp, jnp.zeros((OWN, 128), jnp.float32))
    exp_share = 1.0 / jnp.sum(exp_total, axis=1, keepdims=True)

    wait_for(mrecv.at[pl.ds(1, N_TP - 1)], mrsem)

    def add_own(slot, total):
        amount = mrecv[0, slot].astype(jnp.float32)
        for d in range(1, N_TP):
            amount = amount + mrecv[d, slot].astype(jnp.float32)
        amount = jnp.where(visible_at(slot), amount, 0.0)
        share[slot] = amount
        return total + amount

    def add_side(slot, total):
        amount = jnp.where(visible_at(SLOTS + slot), mside[slot], 0.0)
        share[SLOTS + slot] = amount
        return total + amount

    mass_total = lax.fori_loop(0, SLOTS, add_own, jnp.zeros((OWN, 128), jnp.float32))
    wait_for(mlast, mlsem)
    amount = mlast[0].astype(jnp.float32)
    for d in range(1, N_TP):
        amount = amount + mlast[d].astype(jnp.float32)
    wait_for(mside.at[pl.ds(0, EARLY)], mssem.at[0])
    wait_for(mside.at[pl.ds(EARLY, SLOTS - 1 - EARLY)], mssem.at[1])
    mside[SLOTS - 1] = amount
    mass_total = lax.fori_loop(0, SLOTS, add_side, mass_total)
    mass_total = jnp.sum(mass_total, axis=1, keepdims=True)

    def take_grad(slot, carry):
        lg[slot] = lg[slot] * exp_share - share[slot] / mass_total
        return carry

    lax.fori_loop(0, N_CTX, take_grad, 0)

    def key_pair(pair, carry):
        slot_a, slot_b = 2 * pair, 2 * pair + 1
        keys = jnp.concatenate(
            [
                ikn[source(slot, half), 4 * half : 4 * half + 4].reshape(KEYS // 2, DI)
                for slot in (slot_a, slot_b)
                for half in range(2)
            ],
            axis=0,
        )
        gkt[...] = jnp.zeros_like(gkt)

        def row_block(b, carry):
            first = pl.multiple_of(b * BLOCK, BLOCK)
            pieces = []
            for u in range(BLOCK // HI):
                t = b * (BLOCK // HI) + u
                at = pl.multiple_of(first + u * HI, HI)
                weight = rw_ref[t]
                grad_a = lg[slot_a, pl.ds(t, 1), :] * weight
                grad_b = lg[slot_b, pl.ds(t, 1), :] * weight
                heads = wb[pl.ds(at, HI), :]
                soft_a = nsp[slot_a, pl.ds(at, HI), :]
                soft_b = nsp[slot_b, pl.ds(at, HI), :]
                lanes = pl.ds(pl.multiple_of(FLAT + at, HI), HI)
                nb[0, lanes, :] += grad_a * soft_a + grad_b * soft_b
                part_a = (grad_a * inv_root * heads) * (1.0 - jnp.exp2(soft_a))
                part_b = (grad_b * inv_root * heads) * (1.0 - jnp.exp2(soft_b))
                pieces.append(
                    jnp.concatenate(
                        [part_a.astype(jnp.bfloat16), part_b.astype(jnp.bfloat16)], axis=1
                    )
                )
            score_grad = jnp.concatenate(pieces, axis=0)
            nb[0, pl.ds(first, BLOCK), :] += jnp.dot(
                score_grad, keys, preferred_element_type=jnp.float32
            )
            gkt[...] += jnp.dot(
                iqt[:, pl.ds(first, BLOCK)], score_grad, preferred_element_type=jnp.float32
            )
            return carry

        lax.fori_loop(0, FLAT // BLOCK, row_block, 0, unroll=FLAT // BLOCK)
        at = pl.multiple_of(pair * 2 * KEYS, 2 * KEYS)
        nb[1, pl.ds(at, 2 * KEYS), :] = gkt[...].T
        for part, slot in ((0, slot_a), (1, slot_b)):

            def send(part=part, slot=slot):
                for half in range(2):
                    rows = pl.ds(pl.multiple_of(at + part * KEYS + half * 64, 64), 64)
                    remote(
                        nb.at[1, rows], grk.at[rows], gsend, gsem, ctx=source(slot, half)
                    ).start()

            if part == 0:
                pl.when(pair > 0)(send)
            else:
                send()
        return carry

    lax.fori_loop(0, N_CTX // 2, key_pair, 0)
    out_copy = pltpu.make_async_copy(nb.at[0, pl.ds(0, FLAT)], gq_hbm, osem)
    out_copy.start()

    def finish_weights(r, carry):
        block = nb[0, pl.ds(pl.multiple_of(FLAT + r * 128, 128), 128), :]
        row = jnp.sum(block.T, axis=0, keepdims=True) * -LN2
        gw_ref[pl.ds(2 * r, 1), :] = row[:, :HI]
        gw_ref[pl.ds(2 * r + 1, 1), :] = row[:, HI:]
        return carry

    lax.fori_loop(0, FLAT // 128, finish_weights, 0)

    came = grk.at[pl.ds(KEYS, (N_CTX - 1) * KEYS)]
    wait_for(came, gsem)
    own_sum = nb[1, 0:KEYS, :]
    for slot in range(1, N_CTX):
        own_sum = own_sum + grk[slot * KEYS : (slot + 1) * KEYS, :]
    fst[...] = own_sum.reshape(N_TP, 16, DI)
    for d in range(1, N_TP):
        peer = rem(tp + d, N_TP)
        remote(fst.at[peer], frecv.at[d], fsend, fsem, tp=peer).start()
    landed = frecv.at[pl.ds(1, N_TP - 1)]
    wait_for(landed, fsem)
    total = fst[tp]
    for d in range(1, N_TP):
        total = total + frecv[d]
    gk_ref[...] = total

    out_copy.wait()
    wait_for(landed, fsend)
    wait_for(came, gsend)
    wait_for(kbuf.at[pl.ds(0, SLOTS - 2)], ksend)
    wait_for(kbuf.at[pl.ds(0, 2)], rsend)
    wait_for(qbuf.at[1], qsend)
    wait_for(norm.at[pl.ds(0, 2)], nsend)
    wait_for(ikn.at[pl.ds(0, SIDE - 1), 0], isend.at[0])
    wait_for(ikn.at[pl.ds(0, N_CTX - SIDE), 0], isend.at[1])
    wait_for(ikn.at[:, pl.ds(0, N_TP - 1)], isend.at[2])
    wait_for(gsum.at[pl.ds(0, SLOTS - 1)], mssend)
    wait_for(mlast, dsend)
    wait_for(mrecv.at[pl.ds(0, N_TP - 1)], msend.at[0])
    wait_for(mguest.at[pl.ds(0, N_TP - 1), pl.ds(0, SLOTS - 1)], msend.at[1])


def hand_over(gq_in, gw_in, gk_in, gq_out, gw_out, gk_out, gq, gw, gk, in_sems, out_sems):
    rows = FLAT // PIECES
    pieces = [pl.ds(i * rows, rows) for i in range(PIECES)]
    steps = [(gq_in.at[p], gq.at[p], gq_out.at[p]) for p in pieces]
    steps += [(gw_in, gw, gw_out), (gk_in, gk, gk_out)]
    taken = [pltpu.make_async_copy(a, b, in_sems.at[n]) for n, (a, b, c) in enumerate(steps)]
    given = [pltpu.make_async_copy(b, c, out_sems.at[n]) for n, (a, b, c) in enumerate(steps)]
    for copy in taken:
        copy.start()
    for arrival, copy in zip(taken, given):
        arrival.wait()
        copy.start()
    for copy in given:
        copy.wait()


def per_device(main_q, main_k, log_norms, index_q, index_w, index_k, row_weight, offsets, key_map):
    anywhere = pl.BlockSpec(memory_space=pl.ANY)
    vmem = pl.BlockSpec(memory_space=pltpu.VMEM)
    smem = pl.BlockSpec(memory_space=pltpu.SMEM)
    f32, bf16 = jnp.float32, jnp.bfloat16
    dma = pltpu.SemaphoreType.DMA
    grad_q, grad_w, grad_k = pl.pallas_call(
        kernel,
        out_shape=(
            jax.ShapeDtypeStruct((FLAT, DI), f32),
            jax.ShapeDtypeStruct((OWN, HI), f32),
            jax.ShapeDtypeStruct((16, DI), f32),
        ),
        in_specs=[anywhere, anywhere, anywhere, anywhere, vmem, anywhere, smem, smem, smem],
        out_specs=(anywhere, vmem, vmem),
        scratch_shapes=[
            pltpu.VMEM((2, ROWS, HEADS * DQK), bf16),
            pltpu.VMEM((SLOTS, 2, 4, 16, HEADS * DQK), bf16),
            pltpu.VMEM((2, 4, 16, HEADS * DQK), bf16),
            pltpu.VMEM((N_CTX, N_TP, 16, DI), bf16),
            pltpu.VMEM((FLAT, DI), bf16),
            pltpu.VMEM((DI, FLAT), bf16),
            pltpu.VMEM((3, HEADS, ROWS), f32),
            pltpu.VMEM((2, HEADS * ROWS, 128), f32),
            pltpu.VMEM((FLAT, 128), f32),
            pltpu.VMEM((N_CTX, FLAT, 128), f32),
            pltpu.VMEM((N_CTX, OWN, 128), f32),
            pltpu.VMEM((4 * SLOTS, 4, OWN, 128), bf16),
            pltpu.VMEM((N_TP, SLOTS, OWN, 128), bf16),
            pltpu.VMEM((N_TP, SLOTS, OWN, 128), bf16),
            pltpu.VMEM((SLOTS, OWN, 128), f32),
            pltpu.VMEM((SLOTS, OWN, 128), f32),
            pltpu.VMEM((N_TP, OWN, 128), bf16),
            pltpu.VMEM((N_CTX, OWN, 128), f32),
            pltpu.VMEM((DI, 2 * KEYS), f32),
            pltpu.VMEM((N_CTX * KEYS, DI), f32),
            pltpu.VMEM((N_TP, 16, DI), f32),
            pltpu.VMEM((N_TP, 16, DI), f32),
            dma((5,)),
            dma((SLOTS, 4)),
            dma((4,)),
            dma((4,)),
            dma((2,)),
            dma,
            dma((3,)),
            dma,
            dma((2,)),
            dma((2,)),
            dma,
            dma,
            dma,
            dma,
            dma,
            dma,
            dma,
            dma((3,)),
            dma((2,)),
            dma,
            dma,
            dma,
            dma,
            dma,
        ],
        compiler_params=pltpu.CompilerParams(
            collective_id=0, has_side_effects=True, vmem_limit_bytes=VMEM_LIMIT
        ),
        name="indexer_grads",
    )(
        main_q,
        main_k.reshape(2, 4, 16, HEADS * DQK),
        log_norms.T,
        index_q.reshape(FLAT, DI),
        index_w,
        index_k.reshape(N_TP, 16, DI),
        row_weight,
        offsets,
        key_map,
    )
    grad_q, grad_w, grad_k = pl.pallas_call(
        hand_over,
        out_shape=(
            jax.ShapeDtypeStruct((FLAT, DI), f32),
            jax.ShapeDtypeStruct((OWN, HI), f32),
            jax.ShapeDtypeStruct((16, DI), f32),
        ),
        in_specs=[anywhere] * 3,
        out_specs=(anywhere,) * 3,
        scratch_shapes=[
            pltpu.VMEM((FLAT, DI), f32),
            pltpu.VMEM((OWN, HI), f32),
            pltpu.VMEM((16, DI), f32),
            dma((PIECES + 2,)),
            dma((PIECES + 2,)),
        ],
        name="hand_over",
    )(grad_q, grad_w, grad_k)
    return grad_q.reshape(OWN, HI, DI), grad_w, grad_k


def solution(mesh):
    placed = (
        P("ctx", "tp"),
        P("ctx", "tp"),
        P("ctx", "tp"),
        P(("ctx", "tp"), None, None),
        P(("ctx", "tp"), None),
        P("ctx", None),
        P(("ctx", "tp")),
        P("ctx"),
        P(),
    )
    return jax.shard_map(
        per_device,
        mesh=mesh,
        in_specs=placed,
        out_specs=(P(("ctx", "tp"), None, None), P(("ctx", "tp"), None), P(("ctx", "tp"), None)),
        check_vma=False,
    )
```
